256 devices in a mesh: pb: 64 (over x, y, z_lo), col: 4 (over z_hi, core).
Axes of the slice: x: 4, y: 4, z: 8 (z_hi: 2, z_lo: 4; z = z_hi * 4 + z_lo), core: 2. Of those that a mesh axis runs over, the one named last changes fastest.
Arguments:
- vertex: bfloat16 [3, 256, 448, 896], P(None, 'pb', 'col'), may hold values from -6 to 6
- loop_blocks: bfloat16 [3, 256, 448, 896], P(None, ('pb', 'col')), may hold values from -0.013671875 to 0.013671875
- mixing: float32 [6, 256], replicated, may hold values from -1 to 1
- bond_offsets: int32 [7, 3], replicated, may hold values from -1 to 1
Outputs:
- new_vertex: bfloat16 [3, 256, 448, 896], P(None, 'pb', 'col')
The draws below stay inside these ranges and needn't reach their ends.
All inputs are finite; a program needn't handle non-finite values.
Results may differ from the reference program's by a relative error of at most 0.007.
Values may be sent and summed in bfloat16 or wider, within the bound.
No kernel may reach another device: no remote copies, remote signals or barrier semaphores. Data moves between devices by JAX's collectives and lax.ppermute only.
A program may use at most 64 MiB of HBM per device.

```python
import math
import jax
import jax.numpy as jnp
from jax import lax

NB = 7
N = 448
MX = 8
QD = 4
Q = 256
N_PB = 64


def place_ends(drawn, key, low, high):
    dims = drawn.shape
    spot = [jax.random.randint(jax.random.fold_in(key, axis), (), 0, dims[axis]) for axis in range(len(dims))]
    drawn = drawn.at[tuple(spot)].set(low)
    longest = dims.index(max(dims))
    spot[longest] = (spot[longest] + 1) % dims[longest]
    return drawn.at[tuple(spot)].set(high)


def block_levels(stream_key, shape, shards, low, largest):
    level, own = 1.0, jax.random.fold_in(stream_key, 6)
    for dim, parts in shards:
        draws = jnp.exp(jax.random.uniform(jax.random.fold_in(own, dim), (parts,), jnp.float32, low / len(shards), largest / len(shards)))
        level = level * jnp.repeat(draws, shape[dim] // parts).reshape([-1 if axis == dim else 1 for axis in range(len(shape))])
    return level


def centred(own_key, extent, spread, limit, pieces=(), kind=jnp.bfloat16):
    factor_of = block_levels(own_key, extent, pieces, -0.22, 0.18) if pieces else 1.0
    array = jax.random.normal(own_key, extent, jnp.float32) * spread * factor_of
    return jnp.minimum(jnp.maximum(array, -limit), limit).astype(kind)


def setup_inputs(seed: int = 0) -> dict:
    streams_of = jax.random.split(jax.random.key(seed), 5)
    vertex = centred(streams_of[0], (3, Q, N, 2 * N), 1.0, 6.0, ((1, 64), (2, 4)))
    loop_blocks = centred(streams_of[1], (3, Q, N, 2 * N), (N * N) ** -0.5, 0.013671875, ((1, 256),))
    mixing = jnp.clip(jax.random.uniform(streams_of[2], (6, Q), jnp.float32, -1.0, 1.0), -1.0, 1.0)
    bond_offsets = place_ends(jax.random.randint(streams_of[3], (NB, 3), -1, 2), jax.random.fold_in(streams_of[3], 1), -1, 1).astype(jnp.int32)
    return {"vertex": vertex, "loop_blocks": loop_blocks, "mixing": mixing, "bond_offsets": bond_offsets}


step_length = 0.25


def mesh_coords(momenta, mesh_y, mesh_z):
    flat_index = jnp.arange(momenta, dtype=jnp.int32)
    coord_x = flat_index // (mesh_y * mesh_z)
    coord_y = (flat_index // mesh_z) % mesh_y
    coord_z = flat_index % mesh_z
    return coord_x, coord_y, coord_z


def phase_tables(momenta, mesh_x, mesh_y, mesh_z):
    coord_x, coord_y, coord_z = mesh_coords(momenta, mesh_y, mesh_z)
    phase_index = (coord_x[:, None] * coord_x[None, :] * (mesh_y * mesh_z)
                   + coord_y[:, None] * coord_y[None, :] * (mesh_x * mesh_z)
                   + coord_z[:, None] * coord_z[None, :] * (mesh_x * mesh_y)) % momenta
    angles = phase_index.astype(jnp.float32) * (2.0 * math.pi / momenta)
    cosine = jnp.cos(angles)
    sine_part = jnp.sin(angles)
    forward = jnp.stack([jnp.stack([cosine, sine_part], 1), jnp.stack([-sine_part, cosine], 1)]) * (1.0 / momenta)
    backward = jnp.stack([jnp.stack([cosine, -sine_part], 1), jnp.stack([sine_part, cosine], 1)])
    return forward.astype(jnp.bfloat16), backward.astype(jnp.bfloat16)


def shifted_weights(mixing, bond_offsets, momenta, mesh_x, mesh_y, mesh_z):
    coord_x, coord_y, coord_z = mesh_coords(momenta, mesh_y, mesh_z)
    offsets = (bond_offsets[:, None, :] - bond_offsets[None, :, :]).astype(jnp.int32)
    shift_x = jnp.mod(coord_x[None, None, :] + offsets[:, :, 0:1], mesh_x)
    shift_y = jnp.mod(coord_y[None, None, :] + offsets[:, :, 1:2], mesh_y)
    shift_z = jnp.mod(coord_z[None, None, :] + offsets[:, :, 2:3], mesh_z)
    flat_slot = ((shift_x * mesh_y + shift_y) * mesh_z + shift_z).astype(jnp.int32)
    return jnp.take(mixing, flat_slot, axis=1)


def complex_product(left_op, right_op):
    half_n = left_op.shape[0]
    real_part = jnp.dot(left_op[:, :half_n], right_op, preferred_element_type=jnp.float32)
    imag_part = jnp.dot(left_op[:, half_n:], right_op, preferred_element_type=jnp.float32)
    return jnp.concatenate([real_part[:, :half_n] - imag_part[:, half_n:],
                            real_part[:, half_n:] + imag_part[:, :half_n]], axis=1)


def one_momentum(operands):
    united_q, loop_mat = operands
    middle = complex_product(united_q, loop_mat).astype(jnp.bfloat16)
    return complex_product(middle, united_q)


def reference(vertex, loop_blocks, mixing, bond_offsets):
    momenta = QD * N_PB
    mesh_y = N_PB // MX
    forward, backward = phase_tables(momenta, MX, mesh_y, QD)
    weights = shifted_weights(mixing, bond_offsets, momenta, MX, mesh_y, QD)
    pairs = N // NB
    lattice = []
    for channel in range(3):
        channel_q = vertex[channel].reshape(momenta, N, 2, N).astype(jnp.float32)
        moved = jnp.einsum('qapc,pqsr->rasc', channel_q, forward.astype(jnp.float32)).astype(jnp.bfloat16)
        lattice.append(lax.optimization_barrier(moved).astype(jnp.float32).reshape(momenta, pairs, NB, 2, pairs, NB))
    updated = []
    for target in range(3):
        summed = jnp.zeros((momenta, pairs, NB, 2, pairs, NB), jnp.float32)
        for which in range(2):
            source = (target + 1 + which) % 3
            factor = jnp.transpose(weights[2 * target + which], (2, 0, 1))[:, None, :, None, None, :]
            summed = summed + factor * lattice[source]
        mixed_all = lax.optimization_barrier(summed.astype(jnp.bfloat16)).astype(jnp.float32).reshape(momenta, N, 2, N)
        projected = jnp.einsum('rapc,prsq->qasc', mixed_all, backward.astype(jnp.float32)).astype(jnp.bfloat16)
        projected = lax.optimization_barrier(projected).astype(jnp.float32).reshape(momenta, N, 2 * N)
        united = (vertex[target].astype(jnp.float32) + projected).astype(jnp.bfloat16)
        change = lax.map(one_momentum, (united, loop_blocks[target]))
        increment = lax.optimization_barrier((step_length * change).astype(jnp.bfloat16))
        updated.append((vertex[target].astype(jnp.float32) + increment.astype(jnp.float32)).astype(jnp.bfloat16))
    return jnp.stack(updated)
```

```python
import math

import jax
import jax.numpy as jnp
from jax import lax
from jax.sharding import PartitionSpec as P

NB = 7
MX = 8


step_length = 0.25


def mesh_coords(momenta, mesh_y, mesh_z):
    flat_index = jnp.arange(momenta, dtype=jnp.int32)
    coord_x = flat_index // (mesh_y * mesh_z)
    coord_y = flat_index // mesh_z % mesh_y
    coord_z = flat_index % mesh_z
    return (coord_x, coord_y, coord_z)


def phase_tables(momenta, mesh_x, mesh_y, mesh_z):
    coord_x, coord_y, coord_z = mesh_coords(momenta, mesh_y, mesh_z)
    phase_index = (
        coord_x[:, None] * coord_x[None, :] * (mesh_y * mesh_z)
        + coord_y[:, None] * coord_y[None, :] * (mesh_x * mesh_z)
        + coord_z[:, None] * coord_z[None, :] * (mesh_x * mesh_y)
    ) % momenta
    angles = phase_index.astype(jnp.float32) * (2.0 * math.pi / momenta)
    cosine = jnp.cos(angles)
    sine_part = jnp.sin(angles)
    forward = jnp.stack([jnp.stack([cosine, sine_part], 1), jnp.stack([-sine_part, cosine], 1)]) * (
        1.0 / momenta
    )
    backward = jnp.stack([jnp.stack([cosine, -sine_part], 1), jnp.stack([sine_part, cosine], 1)])
    return (forward.astype(jnp.bfloat16), backward.astype(jnp.bfloat16))


def shifted_weights(mixing, bond_offsets, momenta, mesh_x, mesh_y, mesh_z):
    coord_x, coord_y, coord_z = mesh_coords(momenta, mesh_y, mesh_z)
    offsets = bond_offsets[:, None, :] - bond_offsets[None, :, :]
    shift_x = jnp.mod(coord_x[None, None, :] + offsets[:, :, 0:1], mesh_x)
    shift_y = jnp.mod(coord_y[None, None, :] + offsets[:, :, 1:2], mesh_y)
    shift_z = jnp.mod(coord_z[None, None, :] + offsets[:, :, 2:3], mesh_z)
    flat_slot = (shift_x * mesh_y + shift_y) * mesh_z + shift_z
    return jnp.take(mixing, flat_slot, axis=1)


def per_device(vertex, loop_blocks, mixing, bond_offsets):
    groups = lax.axis_size("pb")
    cols = lax.axis_size("col")
    mesh_z = vertex.shape[1]
    row_count = vertex.shape[2]
    order = vertex.shape[3] // 2
    narrow = order // groups
    momenta = mesh_z * groups
    mesh_y = groups // MX
    forward, backward = phase_tables(momenta, MX, mesh_y, mesh_z)
    weights = shifted_weights(mixing, bond_offsets, momenta, MX, mesh_y, mesh_z)
    split = vertex.reshape(3, mesh_z, row_count, 2, groups, narrow).transpose(4, 1, 3, 0, 5, 2)
    gathered = lax.all_to_all(split, "pb", split_axis=0, concat_axis=0, tiled=True)
    x = gathered.reshape(momenta, 2, 3, narrow, row_count)
    lattice = jnp.einsum("qptna,pqsr->rstna", x, forward, preferred_element_type=jnp.float32)
    lattice = lax.optimization_barrier(lattice.astype(jnp.bfloat16)).astype(jnp.float32)
    w = jnp.tile(weights.transpose(0, 3, 2, 1), (1, 1, 1, row_count // NB))
    mixed = []
    for t in range(3):
        summed = (
            w[2 * t][:, None] * lattice[:, :, (t + 1) % 3]
            + w[2 * t + 1][:, None] * lattice[:, :, (t + 2) % 3]
        )
        mixed.append(summed.astype(jnp.bfloat16))
    mixed = jnp.stack(mixed, axis=2)
    projected = jnp.einsum(
        "rptna,prsq->qstna", mixed, backward, preferred_element_type=jnp.float32
    ).astype(jnp.bfloat16)
    united = (x.astype(jnp.float32) + projected.astype(jnp.float32)).astype(jnp.bfloat16)
    sent = lax.all_to_all(united, ("pb", "col"), split_axis=0, concat_axis=0, tiled=True)
    ut = sent.reshape(groups, cols, 2, 3, narrow, row_count).transpose(3, 2, 0, 4, 1, 5)
    ut = ut.reshape(3, 2, order, order)
    u = ut.transpose(0, 3, 1, 2)
    loops = loop_blocks.reshape(3, order, 2 * order)
    outs = []
    for t in range(3):
        ur, ui = ut[t, 0], ut[t, 1]
        f = lambda l, r: jnp.einsum("ca,cd->ad", l, r, preferred_element_type=jnp.float32)
        re, im = f(ur, loops[t]), f(ui, loops[t])
        m_re = (re[:, :order] - im[:, order:]).astype(jnp.bfloat16)
        m_im = (re[:, order:] + im[:, :order]).astype(jnp.bfloat16)
        g = lambda l, r: jnp.einsum("ad,cd->ac", l, r, preferred_element_type=jnp.float32)
        c_re = g(m_re, ur) - g(m_im, ui)
        c_im = g(m_re, ui) + g(m_im, ur)
        outs.append((step_length * jnp.concatenate([c_re, c_im], axis=1)).astype(jnp.bfloat16))
    increment = jnp.stack(outs, axis=1).reshape(cols, row_count, 3, 2 * order)
    increment = jnp.stack(outs).reshape(3, cols, row_count, 2 * order).transpose(1, 0, 2, 3)
    returned = lax.all_to_all(increment, "col", split_axis=0, concat_axis=0, tiled=True)
    returned = returned.transpose(1, 0, 2, 3)
    return (vertex.astype(jnp.float32) + returned.astype(jnp.float32)).astype(jnp.bfloat16)


def solution(mesh):
    return jax.shard_map(
        per_device,
        mesh=mesh,
        in_specs=(P(None, "pb", "col", None), P(None, ("pb", "col"), None, None), P(), P()),
        out_specs=P(None, "pb", "col", None),
        check_vma=False,
    )
```

```python
import math

import jax
import jax.numpy as jnp
from jax import lax
from jax.sharding import PartitionSpec as P

NB = 7
MX = 8


step_length = 0.25


def mesh_coords(momenta, mesh_y, mesh_z):
    flat_index = jnp.arange(momenta, dtype=jnp.int32)
    coord_x = flat_index // (mesh_y * mesh_z)
    coord_y = flat_index // mesh_z % mesh_y
    coord_z = flat_index % mesh_z
    return (coord_x, coord_y, coord_z)


def phase_tables(momenta, mesh_x, mesh_y, mesh_z):
    coord_x, coord_y, coord_z = mesh_coords(momenta, mesh_y, mesh_z)
    phase_index = (
        coord_x[:, None] * coord_x[None, :] * (mesh_y * mesh_z)
        + coord_y[:, None] * coord_y[None, :] * (mesh_x * mesh_z)
        + coord_z[:, None] * coord_z[None, :] * (mesh_x * mesh_y)
    ) % momenta
    angles = phase_index.astype(jnp.float32) * (2.0 * math.pi / momenta)
    cosine = jnp.cos(angles)
    sine_part = jnp.sin(angles)
    forward = jnp.stack([jnp.stack([cosine, sine_part], 1), jnp.stack([-sine_part, cosine], 1)]) * (
        1.0 / momenta
    )
    backward = jnp.stack([jnp.stack([cosine, -sine_part], 1), jnp.stack([sine_part, cosine], 1)])
    return (forward.astype(jnp.bfloat16), backward.astype(jnp.bfloat16))


def shifted_weights(mixing, bond_offsets, momenta, mesh_x, mesh_y, mesh_z):
    coord_x, coord_y, coord_z = mesh_coords(momenta, mesh_y, mesh_z)
    offsets = bond_offsets[:, None, :] - bond_offsets[None, :, :]
    shift_x = jnp.mod(coord_x[None, None, :] + offsets[:, :, 0:1], mesh_x)
    shift_y = jnp.mod(coord_y[None, None, :] + offsets[:, :, 1:2], mesh_y)
    shift_z = jnp.mod(coord_z[None, None, :] + offsets[:, :, 2:3], mesh_z)
    flat_slot = (shift_x * mesh_y + shift_y) * mesh_z + shift_z
    return jnp.take(mixing, flat_slot, axis=1)


def per_device(vertex, loop_blocks, mixing, bond_offsets):
    groups = lax.axis_size("pb")
    cols = lax.axis_size("col")
    mesh_z = vertex.shape[1]
    row_count = vertex.shape[2]
    order = vertex.shape[3] // 2
    narrow = order // groups
    momenta = mesh_z * groups
    mesh_y = groups // MX
    forward, backward = phase_tables(momenta, MX, mesh_y, mesh_z)
    weights = shifted_weights(mixing, bond_offsets, momenta, MX, mesh_y, mesh_z)
    split = vertex.reshape(3, mesh_z, row_count, 2, groups, narrow).transpose(4, 1, 3, 0, 5, 2)
    gathered = lax.all_to_all(split, "pb", split_axis=0, concat_axis=0, tiled=True)
    x = gathered.reshape(momenta, 2, 3, narrow, row_count)
    lattice = jnp.einsum("qptna,pqsr->rstna", x, forward, preferred_element_type=jnp.float32)
    lattice = lax.optimization_barrier(lattice.astype(jnp.bfloat16)).astype(jnp.float32)
    w = jnp.tile(weights.transpose(0, 3, 2, 1), (1, 1, 1, row_count // NB))
    mixed = []
    for t in range(3):
        summed = (
            w[2 * t][:, None] * lattice[:, :, (t + 1) % 3]
            + w[2 * t + 1][:, None] * lattice[:, :, (t + 2) % 3]
        )
        mixed.append(summed.astype(jnp.bfloat16))
    mixed = jnp.stack(mixed, axis=2)
    projected = jnp.einsum(
        "rptna,prsq->qstna", mixed, backward, preferred_element_type=jnp.float32
    ).astype(jnp.bfloat16)
    united = (x.astype(jnp.float32) + projected.astype(jnp.float32)).astype(jnp.bfloat16)
    sent = lax.all_to_all(united, ("pb", "col"), split_axis=0, concat_axis=0, tiled=True)
    ut = sent.reshape(groups, cols, 2, 3, narrow, row_count).transpose(3, 2, 0, 4, 1, 5)
    ut = ut.reshape(3, 2, order, order)
    u = ut.transpose(0, 3, 1, 2)
    loops = loop_blocks.reshape(3, order, 2 * order)
    mine = lax.axis_index("col")
    outs = []
    for t in range(3):
        ur, ui, loop = ut[t, 0], ut[t, 1], loops[t]
        if t:
            ur, ui, loop, increment = lax.optimization_barrier((ur, ui, loop, increment))
        f = lambda l, r: jnp.einsum("ca,cd->ad", l, r, preferred_element_type=jnp.float32)
        re, im = f(ur, loop), f(ui, loop)
        m_re = (re[:, :order] - im[:, order:]).astype(jnp.bfloat16)
        m_im = (re[:, order:] + im[:, :order]).astype(jnp.bfloat16)
        g = lambda l, r: jnp.einsum("ad,cd->ac", l, r, preferred_element_type=jnp.float32)
        c_re = g(m_re, ur) - g(m_im, ui)
        c_im = g(m_re, ui) + g(m_im, ur)
        increment = (step_length * jnp.concatenate([c_re, c_im], axis=1)).astype(jnp.bfloat16)
        increment = increment.reshape(cols, row_count, 2 * order)
        pieces = []
        for k in range(cols):
            piece = lax.dynamic_index_in_dim(increment, mine ^ k, 0, keepdims=False)
            if k:
                piece = lax.ppermute(piece, "col", [(i, i ^ k) for i in range(cols)])
            pieces.append(piece)
        low, high = (mine & 1) == 1, (mine & 2) == 2
        a, b, c, d = pieces
        a, b = jnp.where(low, b, a), jnp.where(low, a, b)
        c, d = jnp.where(low, d, c), jnp.where(low, c, d)
        a, c = jnp.where(high, c, a), jnp.where(high, a, c)
        b, d = jnp.where(high, d, b), jnp.where(high, b, d)
        returned = jnp.stack([a, b, c, d])
        outs.append(
            (vertex[t].astype(jnp.float32) + returned.astype(jnp.float32)).astype(jnp.bfloat16)
        )
    return jnp.stack(outs)


def solution(mesh):
    return jax.shard_map(
        per_device,
        mesh=mesh,
        in_specs=(P(None, "pb", "col", None), P(None, ("pb", "col"), None, None), P(), P()),
        out_specs=P(None, "pb", "col", None),
        check_vma=False,
    )
```

```python
import math

import jax
import jax.numpy as jnp
from jax import lax
from jax.experimental import pallas as pl
from jax.experimental.pallas import tpu as pltpu
from jax.sharding import PartitionSpec as P

NB = 7
MX = 8
LANES = 128


step_length = 0.25


def mesh_coords(momenta, mesh_y, mesh_z):
    flat_index = jnp.arange(momenta, dtype=jnp.int32)
    coord_x = flat_index // (mesh_y * mesh_z)
    coord_y = flat_index // mesh_z % mesh_y
    coord_z = flat_index % mesh_z
    return (coord_x, coord_y, coord_z)


def phase_tables(momenta, mesh_x, mesh_y, mesh_z):
    coord_x, coord_y, coord_z = mesh_coords(momenta, mesh_y, mesh_z)
    phase_index = (
        coord_x[:, None] * coord_x[None, :] * (mesh_y * mesh_z)
        + coord_y[:, None] * coord_y[None, :] * (mesh_x * mesh_z)
        + coord_z[:, None] * coord_z[None, :] * (mesh_x * mesh_y)
    ) % momenta
    angles = phase_index.astype(jnp.float32) * (2.0 * math.pi / momenta)
    cosine = jnp.cos(angles)
    sine_part = jnp.sin(angles)
    forward = jnp.stack([jnp.stack([cosine, sine_part], 1), jnp.stack([-sine_part, cosine], 1)]) * (
        1.0 / momenta
    )
    backward = jnp.stack([jnp.stack([cosine, -sine_part], 1), jnp.stack([sine_part, cosine], 1)])
    return (forward.astype(jnp.bfloat16), backward.astype(jnp.bfloat16))


def pieces_of(values, axis):
    high = lax.reduce_precision(values, 8, 7)
    rest = values - high
    middle = lax.reduce_precision(rest, 8, 7)
    return jnp.concatenate([high, middle, rest - middle], axis=axis).astype(jnp.bfloat16)


def shifted_slots(bond_offsets, sign, sides):
    mesh_x, mesh_y, mesh_z = sides
    coords = mesh_coords(mesh_x * mesh_y * mesh_z, mesh_y, mesh_z)
    slot = 0
    for axis, side in enumerate(sides):
        moved = jnp.mod(coords[axis][None, :] + sign * bond_offsets[:, axis][:, None], side)
        slot = slot * side + moved
    return slot


def shifted_weights(mixing, bond_offsets, column_bonds, row_count, sides):
    count, momenta = mixing.shape
    f32 = jnp.float32
    slots = shifted_slots(bond_offsets, 1, sides)
    source = lax.broadcasted_iota(jnp.int32, (momenta, NB, momenta), 0)
    picks = (source == slots[None]).astype(jnp.bfloat16).reshape(momenta, NB * momenta)
    first = jnp.dot(pieces_of(mixing, 0), picks, preferred_element_type=f32)
    first = first[:count] + first[count : 2 * count] + first[2 * count :]
    first = first.reshape(count * NB, momenta)
    row = lax.broadcasted_iota(jnp.int32, (count * NB, count * LANES), 0)
    lane = lax.broadcasted_iota(jnp.int32, (count * NB, count * LANES), 1)
    spot = lane % LANES
    spread = (row == lane // LANES * NB + spot % NB) & (spot < row_count)
    spread = spread.astype(jnp.bfloat16)
    wide = jnp.dot(pieces_of(first.T, 0), spread, preferred_element_type=f32)
    wide = wide[:momenta] + wide[momenta : 2 * momenta] + wide[2 * momenta :]
    slots = shifted_slots(column_bonds, -1, sides).reshape(NB * momenta)
    target = lax.broadcasted_iota(jnp.int32, (NB * momenta, momenta), 1)
    picks = (target == slots[:, None]).astype(jnp.bfloat16)
    both = jnp.dot(picks, pieces_of(wide, 1), preferred_element_type=f32)
    width = count * LANES
    both = both[:, :width] + both[:, width : 2 * width] + both[:, 2 * width :]
    return both.reshape(NB, momenta, width)


def spread_kernel(v_ref, out_ref, tmp_ref):
    _, mesh_z, row_count, width = v_ref.shape
    groups = out_ref.shape[0]
    narrow = out_ref.shape[1]
    order = width // 2
    for z in range(mesh_z):
        block = v_ref[0, z].astype(jnp.float32)
        block = jnp.concatenate([block, jnp.zeros((LANES - row_count, width), jnp.float32)], axis=0)
        turned = block.T
        for p in range(2):
            for n in range(narrow):
                start = p * order + n * groups
                tmp_ref[n, pl.ds(2 * z + p, groups, stride=2 * mesh_z), :] = turned[
                    start : start + groups
                ]
    for n in range(narrow):
        out_ref[:, n] = tmp_ref[n].reshape(groups, 2 * mesh_z, LANES).astype(jnp.bfloat16)


def spread_rows(vertex, groups):
    _, mesh_z, row_count, width = vertex.shape
    narrow = width // 2 // groups
    return pl.pallas_call(
        spread_kernel,
        grid=(3,),
        in_specs=[pl.BlockSpec((1, mesh_z, row_count, width), lambda t: (t, 0, 0, 0))],
        out_specs=pl.BlockSpec((groups, narrow, 2 * mesh_z, LANES), lambda t: (0, t, 0, 0)),
        out_shape=jax.ShapeDtypeStruct((groups, 3 * narrow, 2 * mesh_z, LANES), jnp.bfloat16),
        scratch_shapes=[pltpu.VMEM((narrow, groups * 2 * mesh_z, LANES), jnp.float32)],
        compiler_params=pltpu.CompilerParams(vmem_limit_bytes=32 * 1024 * 1024),
    )(vertex)


def transform_kernel(x_ref, forward_ref, backward_ref, w_ref, out_ref):
    f32, bf16 = jnp.float32, jnp.bfloat16
    rows = forward_ref.shape[0]
    momenta = rows // 2
    x = [x_ref[:, t, 0].astype(f32).reshape(rows, LANES) for t in range(3)]
    x_all = jnp.concatenate([part.astype(bf16) for part in x], axis=1)
    lattice = jnp.dot(forward_ref[...], x_all, preferred_element_type=f32).astype(bf16).astype(f32)
    mixed = []
    for t in range(3):
        first = lattice[:, (t + 1) % 3 * LANES : ((t + 1) % 3 + 1) * LANES]
        second = lattice[:, (t + 2) % 3 * LANES : ((t + 2) % 3 + 1) * LANES]
        w1 = w_ref[0, :, 2 * t * LANES : (2 * t + 1) * LANES]
        w2 = w_ref[0, :, (2 * t + 1) * LANES : (2 * t + 2) * LANES]
        halves = [
            w1 * first[s * momenta : (s + 1) * momenta] + w2 * second[s * momenta : (s + 1) * momenta]
            for s in range(2)
        ]
        mixed.append(jnp.concatenate(halves, axis=0).astype(bf16))
    mixed = jnp.concatenate(mixed, axis=1)
    projected = jnp.dot(backward_ref[...], mixed, preferred_element_type=f32).astype(bf16)
    for t in range(3):
        part = projected[:, t * LANES : (t + 1) * LANES].astype(f32)
        out_ref[t, 0] = (x[t] + part).astype(bf16)


def transform(x, forward, backward, w):
    groups, _, narrow, inner, _ = x.shape
    rows = groups * inner
    width = w.shape[2]
    return pl.pallas_call(
        transform_kernel,
        grid=(narrow,),
        in_specs=[
            pl.BlockSpec((groups, 3, 1, inner, LANES), lambda n: (0, 0, n, 0, 0)),
            pl.BlockSpec((rows, rows), lambda n: (0, 0)),
            pl.BlockSpec((rows, rows), lambda n: (0, 0)),
            pl.BlockSpec((1, rows // 2, width), lambda n: (n, 0, 0)),
        ],
        out_specs=pl.BlockSpec((3, 1, rows, LANES), lambda n: (0, n, 0, 0)),
        out_shape=jax.ShapeDtypeStruct((3, narrow, rows, LANES), jnp.bfloat16),
        compiler_params=pltpu.CompilerParams(vmem_limit_bytes=32 * 1024 * 1024),
    )(x, forward, backward, w)


def products_kernel(u_ref, loop_ref, out_ref, tall_ref, wide_ref):
    f32, bf16 = jnp.float32, jnp.bfloat16
    narrow, _, cols, groups, _ = u_ref.shape
    order = narrow * groups
    depth = cols * LANES
    row_count = out_ref.shape[1]
    for n in range(narrow):
        for k in range(cols):
            rows, lanes = n * groups, k * LANES
            real, imag = u_ref[n, 0, k], u_ref[n, 1, k]
            tall_ref[rows : rows + groups, lanes : lanes + LANES] = real
            tall_ref[order + rows : order + rows + groups, lanes : lanes + LANES] = imag
            wide_ref[rows : rows + groups, lanes : lanes + LANES] = real
            wide_ref[rows : rows + groups, depth + lanes : depth + lanes + LANES] = -imag
            wide_ref[order + rows : order + rows + groups, lanes : lanes + LANES] = imag
            wide_ref[order + rows : order + rows + groups, depth + lanes : depth + lanes + LANES] = real
    middle = lax.dot_general(
        tall_ref[...], loop_ref[0], (((0,), (0,)), ((), ())), preferred_element_type=f32
    ).astype(bf16)
    change = lax.dot_general(
        middle, wide_ref[...], (((1,), (1,)), ((), ())), preferred_element_type=f32
    )
    increment = (step_length * change).astype(bf16)
    for k in range(cols):
        out_ref[k] = increment[k * LANES : k * LANES + row_count]


def products(t, u, loops, row_count):
    _, _, cols, groups, _ = u.shape
    narrow = u.shape[0] // 3
    rows, depth = loops.shape[1:]
    return pl.pallas_call(
        products_kernel,
        grid=(1,),
        in_specs=[
            pl.BlockSpec((narrow, 2, cols, groups, LANES), lambda i: (t, 0, 0, 0, 0)),
            pl.BlockSpec((1, rows, depth), lambda i: (t, 0, 0)),
        ],
        out_specs=pl.BlockSpec((cols, row_count, rows), lambda i: (0, 0, 0)),
        out_shape=jax.ShapeDtypeStruct((cols, row_count, rows), jnp.bfloat16),
        scratch_shapes=[
            pltpu.VMEM((rows, depth // 2), jnp.bfloat16),
            pltpu.VMEM((rows, depth), jnp.bfloat16),
        ],
        compiler_params=pltpu.CompilerParams(vmem_limit_bytes=32 * 1024 * 1024),
    )(u, loops)


def per_device(vertex, loop_blocks, mixing, bond_offsets):
    groups = lax.axis_size("pb")
    cols = lax.axis_size("col")
    mesh_z = vertex.shape[1]
    row_count = vertex.shape[2]
    order = vertex.shape[3] // 2
    narrow = order // groups
    momenta = mesh_z * groups
    mesh_y = groups // MX
    sent = spread_rows(vertex, groups)
    gathered = lax.all_to_all(sent, "pb", split_axis=0, concat_axis=0, tiled=True)

    forward, backward = phase_tables(momenta, MX, mesh_y, mesh_z)
    forward = forward.transpose(2, 3, 1, 0).reshape(2 * momenta, 2 * momenta)
    backward = backward.transpose(3, 2, 0, 1).reshape(2 * momenta, 2 * momenta)
    bond = jnp.arange(NB, dtype=jnp.int32)
    own = (jnp.arange(narrow, dtype=jnp.int32) * groups + lax.axis_index("pb")) % NB
    column_bonds = jnp.sum(
        jnp.where((own[:, None] == bond[None, :])[:, :, None], bond_offsets[None], 0), axis=1
    )
    w = shifted_weights(mixing, bond_offsets, column_bonds, row_count, (MX, mesh_y, mesh_z))
    lane_pad = LANES - row_count
    loops = loop_blocks.reshape(3, order, 2, cols, row_count)
    loops = jnp.pad(loops, [(0, 0)] * 4 + [(0, lane_pad)]).reshape(3, order, 2, cols * LANES)
    loop_re, loop_im = loops[:, :, 0], loops[:, :, 1]
    loops = jnp.concatenate(
        [
            jnp.concatenate([loop_re, loop_im], axis=2),
            jnp.concatenate([-loop_im, loop_re], axis=2),
        ],
        axis=1,
    )

    gathered = gathered.reshape(groups, 3, narrow, 2 * mesh_z, LANES)
    united = transform(gathered, forward, backward, w)
    united = united.reshape(3 * narrow, momenta, 2, LANES).transpose(1, 0, 2, 3)
    sent = lax.all_to_all(united, ("pb", "col"), split_axis=0, concat_axis=0, tiled=True)
    u = sent.reshape(groups, cols, 3 * narrow, 2, LANES).transpose(2, 3, 1, 0, 4)
    mine = lax.axis_index("col")
    outs = []
    for t in range(3):
        increment = products(t, u, loops, row_count)
        pieces = []
        for k in range(cols):
            piece = lax.dynamic_index_in_dim(increment, mine ^ k, 0, keepdims=False)
            if k:
                piece = lax.ppermute(piece, "col", [(i, i ^ k) for i in range(cols)])
            pieces.append(piece)
        low, high = (mine & 1) == 1, (mine & 2) == 2
        a, b, c, d = pieces
        a, b = jnp.where(low, b, a), jnp.where(low, a, b)
        c, d = jnp.where(low, d, c), jnp.where(low, c, d)
        a, c = jnp.where(high, c, a), jnp.where(high, a, c)
        b, d = jnp.where(high, d, b), jnp.where(high, b, d)
        returned = jnp.stack([a, b, c, d])
        outs.append(
            (vertex[t].astype(jnp.float32) + returned.astype(jnp.float32)).astype(jnp.bfloat16)
        )
    return jnp.stack(outs)


def solution(mesh):
    return jax.shard_map(
        per_device,
        mesh=mesh,
        in_specs=(P(None, "pb", "col", None), P(None, ("pb", "col"), None, None), P(), P()),
        out_specs=P(None, "pb", "col", None),
        check_vma=False,
    )
```

```python
import functools
import math

import jax
import jax.numpy as jnp
from jax import lax
from jax.experimental import pallas as pl
from jax.experimental.pallas import tpu as pltpu
from jax.sharding import PartitionSpec as P

NB = 7
MX = 8
LANES = 128


step_length = 0.25


def mesh_coords(momenta, mesh_y, mesh_z):
    flat_index = jnp.arange(momenta, dtype=jnp.int32)
    coord_x = flat_index // (mesh_y * mesh_z)
    coord_y = flat_index // mesh_z % mesh_y
    coord_z = flat_index % mesh_z
    return (coord_x, coord_y, coord_z)


def phase_tables(momenta, mesh_x, mesh_y, mesh_z):
    coord_x, coord_y, coord_z = mesh_coords(momenta, mesh_y, mesh_z)
    phase_index = (
        coord_x[:, None] * coord_x[None, :] * (mesh_y * mesh_z)
        + coord_y[:, None] * coord_y[None, :] * (mesh_x * mesh_z)
        + coord_z[:, None] * coord_z[None, :] * (mesh_x * mesh_y)
    ) % momenta
    angles = phase_index.astype(jnp.float32) * (2.0 * math.pi / momenta)
    cosine = jnp.cos(angles)
    sine_part = jnp.sin(angles)
    forward = jnp.stack([jnp.stack([cosine, sine_part], 1), jnp.stack([-sine_part, cosine], 1)]) * (
        1.0 / momenta
    )
    backward = jnp.stack([jnp.stack([cosine, -sine_part], 1), jnp.stack([sine_part, cosine], 1)])
    return (forward.astype(jnp.bfloat16), backward.astype(jnp.bfloat16))


def pieces_of(values, axis):
    high = lax.reduce_precision(values, 8, 7)
    rest = values - high
    middle = lax.reduce_precision(rest, 8, 7)
    return jnp.concatenate([high, middle, rest - middle], axis=axis).astype(jnp.bfloat16)


def shifted_slots(bond_offsets, sign, sides):
    mesh_x, mesh_y, mesh_z = sides
    coords = mesh_coords(mesh_x * mesh_y * mesh_z, mesh_y, mesh_z)
    slot = 0
    for axis, side in enumerate(sides):
        moved = jnp.mod(coords[axis][None, :] + sign * bond_offsets[:, axis][:, None], side)
        slot = slot * side + moved
    return slot


def shifted_weights(mixing, bond_offsets, column_bonds, row_count, sides):
    count, momenta = mixing.shape
    f32 = jnp.float32
    slots = shifted_slots(bond_offsets, 1, sides)
    source = lax.broadcasted_iota(jnp.int32, (momenta, NB, momenta), 0)
    picks = (source == slots[None]).astype(jnp.bfloat16).reshape(momenta, NB * momenta)
    first = jnp.dot(pieces_of(mixing, 0), picks, preferred_element_type=f32)
    first = first[:count] + first[count : 2 * count] + first[2 * count :]
    first = first.reshape(count * NB, momenta)
    row = lax.broadcasted_iota(jnp.int32, (count * NB, count * LANES), 0)
    lane = lax.broadcasted_iota(jnp.int32, (count * NB, count * LANES), 1)
    spot = lane % LANES
    spread = (row == lane // LANES * NB + spot % NB) & (spot < row_count)
    spread = spread.astype(jnp.bfloat16)
    wide = jnp.dot(pieces_of(first.T, 0), spread, preferred_element_type=f32)
    wide = wide[:momenta] + wide[momenta : 2 * momenta] + wide[2 * momenta :]
    slots = shifted_slots(column_bonds, -1, sides).reshape(NB * momenta)
    target = lax.broadcasted_iota(jnp.int32, (NB * momenta, momenta), 1)
    picks = (target == slots[:, None]).astype(jnp.bfloat16)
    both = jnp.dot(picks, pieces_of(wide, 1), preferred_element_type=f32)
    width = count * LANES
    both = both[:, :width] + both[:, width : 2 * width] + both[:, 2 * width :]
    return both.reshape(NB, momenta, width)


def spread_kernel(v_ref, out_ref, tmp_ref):
    _, mesh_z, row_count, width = v_ref.shape
    groups = out_ref.shape[0]
    narrow = out_ref.shape[1]
    order = width // 2
    for z in range(mesh_z):
        block = v_ref[0, z].astype(jnp.float32)
        block = jnp.concatenate([block, jnp.zeros((LANES - row_count, width), jnp.float32)], axis=0)
        turned = block.T
        for p in range(2):
            for n in range(narrow):
                start = p * order + n * groups
                tmp_ref[n, pl.ds(2 * z + p, groups, stride=2 * mesh_z), :] = turned[
                    start : start + groups
                ]
    for n in range(narrow):
        out_ref[:, n] = tmp_ref[n].reshape(groups, 2 * mesh_z, LANES).astype(jnp.bfloat16)


def spread_rows(vertex, groups):
    _, mesh_z, row_count, width = vertex.shape
    narrow = width // 2 // groups
    return pl.pallas_call(
        spread_kernel,
        grid=(3,),
        in_specs=[pl.BlockSpec((1, mesh_z, row_count, width), lambda t: (t, 0, 0, 0))],
        out_specs=pl.BlockSpec((groups, narrow, 2 * mesh_z, LANES), lambda t: (0, t, 0, 0)),
        out_shape=jax.ShapeDtypeStruct((groups, 3 * narrow, 2 * mesh_z, LANES), jnp.bfloat16),
        scratch_shapes=[pltpu.VMEM((narrow, groups * 2 * mesh_z, LANES), jnp.float32)],
        compiler_params=pltpu.CompilerParams(vmem_limit_bytes=32 * 1024 * 1024),
    )(in_hbm(vertex))


def transform_kernel(t, x_ref, forward_ref, backward_ref, w_ref, out_ref):
    f32, bf16 = jnp.float32, jnp.bfloat16
    rows = forward_ref.shape[0]
    momenta = rows // 2
    x = [x_ref[:, i, 0].astype(f32).reshape(rows, LANES) for i in range(3)]
    pair = jnp.concatenate([x[(t + 1) % 3].astype(bf16), x[(t + 2) % 3].astype(bf16)], axis=1)
    lattice = jnp.dot(forward_ref[...], pair, preferred_element_type=f32).astype(bf16).astype(f32)
    halves = []
    for s in range(2):
        half = lattice[s * momenta : (s + 1) * momenta]
        halves.append(
            w_ref[0, :, :LANES] * half[:, :LANES] + w_ref[0, :, LANES:] * half[:, LANES:]
        )
    mixed = jnp.concatenate(halves, axis=0).astype(bf16)
    projected = jnp.dot(backward_ref[...], mixed, preferred_element_type=f32).astype(bf16)
    out_ref[0] = (x[t] + projected.astype(f32)).astype(bf16)


def in_hbm(array):
    return pltpu.with_memory_space_constraint(array, pltpu.HBM)


def transform(t, x, forward, backward, w):
    groups, _, narrow, inner, _ = x.shape
    rows = groups * inner
    return pl.pallas_call(
        functools.partial(transform_kernel, t),
        grid=(narrow,),
        in_specs=[
            pl.BlockSpec((groups, 3, 1, inner, LANES), lambda n: (0, 0, n, 0, 0)),
            pl.BlockSpec((rows, rows), lambda n: (0, 0)),
            pl.BlockSpec((rows, rows), lambda n: (0, 0)),
            pl.BlockSpec((1, rows // 2, 2 * LANES), lambda n: (n, 0, t)),
        ],
        out_specs=pl.BlockSpec((1, rows, LANES), lambda n: (n, 0, 0)),
        out_shape=jax.ShapeDtypeStruct((narrow, rows, LANES), jnp.bfloat16),
        compiler_params=pltpu.CompilerParams(vmem_limit_bytes=32 * 1024 * 1024),
    )(x, forward, backward, in_hbm(w))


def products_kernel(u_ref, loop_ref, out_ref, tall_ref, wide_ref):
    f32, bf16 = jnp.float32, jnp.bfloat16
    narrow, _, cols, groups, _ = u_ref.shape
    order = narrow * groups
    depth = cols * LANES
    row_count = out_ref.shape[1]
    for n in range(narrow):
        for k in range(cols):
            rows, lanes = n * groups, k * LANES
            real, imag = u_ref[n, 0, k], u_ref[n, 1, k]
            tall_ref[rows : rows + groups, lanes : lanes + LANES] = real
            tall_ref[order + rows : order + rows + groups, lanes : lanes + LANES] = imag
            wide_ref[rows : rows + groups, lanes : lanes + LANES] = real
            wide_ref[rows : rows + groups, depth + lanes : depth + lanes + LANES] = -imag
            wide_ref[order + rows : order + rows + groups, lanes : lanes + LANES] = imag
            wide_ref[order + rows : order + rows + groups, depth + lanes : depth + lanes + LANES] = real
    middle = lax.dot_general(
        tall_ref[...], loop_ref[0], (((0,), (0,)), ((), ())), preferred_element_type=f32
    ).astype(bf16)
    change = lax.dot_general(
        middle, wide_ref[...], (((1,), (1,)), ((), ())), preferred_element_type=f32
    )
    increment = (step_length * change).astype(bf16)
    for k in range(cols):
        out_ref[k] = increment[k * LANES : k * LANES + row_count]


def products(t, u, loops, row_count):
    _, _, cols, groups, _ = u.shape
    narrow = u.shape[0]
    rows, depth = loops.shape[1:]
    return pl.pallas_call(
        products_kernel,
        grid=(1,),
        in_specs=[
            pl.BlockSpec((narrow, 2, cols, groups, LANES), lambda i: (0, 0, 0, 0, 0)),
            pl.BlockSpec((1, rows, depth), lambda i: (t, 0, 0)),
        ],
        out_specs=pl.BlockSpec((cols, row_count, rows), lambda i: (0, 0, 0)),
        out_shape=jax.ShapeDtypeStruct((cols, row_count, rows), jnp.bfloat16),
        scratch_shapes=[
            pltpu.VMEM((rows, depth // 2), jnp.bfloat16),
            pltpu.VMEM((rows, depth), jnp.bfloat16),
        ],
        compiler_params=pltpu.CompilerParams(vmem_limit_bytes=32 * 1024 * 1024),
    )(u, in_hbm(loops))


def per_device(vertex, loop_blocks, mixing, bond_offsets):
    groups = lax.axis_size("pb")
    cols = lax.axis_size("col")
    mesh_z = vertex.shape[1]
    row_count = vertex.shape[2]
    order = vertex.shape[3] // 2
    narrow = order // groups
    momenta = mesh_z * groups
    mesh_y = groups // MX
    sent = spread_rows(vertex, groups)
    gathered = lax.all_to_all(sent, "pb", split_axis=0, concat_axis=0, tiled=True)

    forward, backward = phase_tables(momenta, MX, mesh_y, mesh_z)
    forward = forward.transpose(2, 3, 1, 0).reshape(2 * momenta, 2 * momenta)
    backward = backward.transpose(3, 2, 0, 1).reshape(2 * momenta, 2 * momenta)
    bond = jnp.arange(NB, dtype=jnp.int32)
    own = (jnp.arange(narrow, dtype=jnp.int32) * groups + lax.axis_index("pb")) % NB
    column_bonds = jnp.sum(
        jnp.where((own[:, None] == bond[None, :])[:, :, None], bond_offsets[None], 0), axis=1
    )
    w = shifted_weights(mixing, bond_offsets, column_bonds, row_count, (MX, mesh_y, mesh_z))
    lane_pad = LANES - row_count
    loops = loop_blocks.reshape(3, order, 2, cols, row_count)
    loops = jnp.pad(loops, [(0, 0)] * 4 + [(0, lane_pad)]).reshape(3, order, 2, cols * LANES)
    loop_re, loop_im = loops[:, :, 0], loops[:, :, 1]
    loops = jnp.concatenate(
        [
            jnp.concatenate([loop_re, loop_im], axis=2),
            jnp.concatenate([-loop_im, loop_re], axis=2),
        ],
        axis=1,
    )

    gathered, w, loops = lax.optimization_barrier((gathered, w, loops))
    gathered = gathered.reshape(groups, 3, narrow, 2 * mesh_z, LANES)
    mine = lax.axis_index("col")
    outs = []
    for t in range(3):
        united = transform(t, gathered, forward, backward, w)
        united = united.reshape(narrow, momenta, 2, LANES).transpose(1, 0, 2, 3)
        sent = lax.all_to_all(united, ("pb", "col"), split_axis=0, concat_axis=0, tiled=True)
        u = sent.reshape(groups, cols, narrow, 2, LANES).transpose(2, 3, 1, 0, 4)
        increment = products(t, u, loops, row_count)
        pieces = []
        for k in range(cols):
            piece = lax.dynamic_index_in_dim(increment, mine ^ k, 0, keepdims=False)
            if k:
                piece = lax.ppermute(piece, "col", [(i, i ^ k) for i in range(cols)])
            pieces.append(piece)
        low, high = (mine & 1) == 1, (mine & 2) == 2
        a, b, c, d = pieces
        a, b = jnp.where(low, b, a), jnp.where(low, a, b)
        c, d = jnp.where(low, d, c), jnp.where(low, c, d)
        a, c = jnp.where(high, c, a), jnp.where(high, a, c)
        b, d = jnp.where(high, d, b), jnp.where(high, b, d)
        returned = jnp.stack([a, b, c, d])
        outs.append(
            (vertex[t].astype(jnp.float32) + returned.astype(jnp.float32)).astype(jnp.bfloat16)
        )
    return jnp.stack(outs)


def solution(mesh):
    return jax.shard_map(
        per_device,
        mesh=mesh,
        in_specs=(P(None, "pb", "col", None), P(None, ("pb", "col"), None, None), P(), P()),
        out_specs=P(None, "pb", "col", None),
        check_vma=False,
    )
```

```python
import functools
import math

import jax
import jax.numpy as jnp
from jax import lax
from jax.experimental import pallas as pl
from jax.experimental.pallas import tpu as pltpu
from jax.sharding import PartitionSpec as P

NB = 7
MX = 8
LANES = 128


step_length = 0.25


def mesh_coords(momenta, mesh_y, mesh_z):
    flat_index = jnp.arange(momenta, dtype=jnp.int32)
    coord_x = flat_index // (mesh_y * mesh_z)
    coord_y = flat_index // mesh_z % mesh_y
    coord_z = flat_index % mesh_z
    return (coord_x, coord_y, coord_z)


def phase_tables(momenta, mesh_x, mesh_y, mesh_z):
    coord_x, coord_y, coord_z = mesh_coords(momenta, mesh_y, mesh_z)
    phase_index = (
        coord_x[:, None] * coord_x[None, :] * (mesh_y * mesh_z)
        + coord_y[:, None] * coord_y[None, :] * (mesh_x * mesh_z)
        + coord_z[:, None] * coord_z[None, :] * (mesh_x * mesh_y)
    ) % momenta
    angles = phase_index.astype(jnp.float32) * (2.0 * math.pi / momenta)
    cosine = jnp.cos(angles)
    sine_part = jnp.sin(angles)
    forward = jnp.stack([jnp.stack([cosine, sine_part], 1), jnp.stack([-sine_part, cosine], 1)]) * (
        1.0 / momenta
    )
    backward = jnp.stack([jnp.stack([cosine, -sine_part], 1), jnp.stack([sine_part, cosine], 1)])
    return (forward.astype(jnp.bfloat16), backward.astype(jnp.bfloat16))


def pieces_of(values, axis):
    high = lax.reduce_precision(values, 8, 7)
    rest = values - high
    middle = lax.reduce_precision(rest, 8, 7)
    return jnp.concatenate([high, middle, rest - middle], axis=axis).astype(jnp.bfloat16)


def shifted_slots(bond_offsets, sign, sides):
    mesh_x, mesh_y, mesh_z = sides
    coords = mesh_coords(mesh_x * mesh_y * mesh_z, mesh_y, mesh_z)
    slot = 0
    for axis, side in enumerate(sides):
        moved = jnp.mod(coords[axis][None, :] + sign * bond_offsets[:, axis][:, None], side)
        slot = slot * side + moved
    return slot


def shifted_weights(mixing, bond_offsets, column_bonds, row_count, sides):
    count, momenta = mixing.shape
    f32 = jnp.float32
    slots = shifted_slots(bond_offsets, 1, sides)
    source = lax.broadcasted_iota(jnp.int32, (momenta, NB, momenta), 0)
    picks = (source == slots[None]).astype(jnp.bfloat16).reshape(momenta, NB * momenta)
    first = jnp.dot(pieces_of(mixing, 0), picks, preferred_element_type=f32)
    first = first[:count] + first[count : 2 * count] + first[2 * count :]
    first = first.reshape(count * NB, momenta)
    row = lax.broadcasted_iota(jnp.int32, (count * NB, count * LANES), 0)
    lane = lax.broadcasted_iota(jnp.int32, (count * NB, count * LANES), 1)
    spot = lane % LANES
    spread = (row == lane // LANES * NB + spot % NB) & (spot < row_count)
    spread = spread.astype(jnp.bfloat16)
    wide = jnp.dot(pieces_of(first.T, 0), spread, preferred_element_type=f32)
    wide = wide[:momenta] + wide[momenta : 2 * momenta] + wide[2 * momenta :]
    slots = shifted_slots(column_bonds, -1, sides).reshape(NB * momenta)
    target = lax.broadcasted_iota(jnp.int32, (NB * momenta, momenta), 1)
    picks = (target == slots[:, None]).astype(jnp.bfloat16)
    both = jnp.dot(picks, pieces_of(wide, 1), preferred_element_type=f32)
    width = count * LANES
    both = both[:, :width] + both[:, width : 2 * width] + both[:, 2 * width :]
    both = both.reshape(NB, momenta, count, LANES)[..., :row_count]
    both = both.transpose(2, 1, 0, 3).reshape(count, momenta, NB * row_count)
    short = -(NB * row_count) % LANES
    return jnp.pad(both, ((0, 0), (0, 0), (0, short)))


def lane_ids(rows):
    return lax.broadcasted_iota(jnp.int32, (rows, LANES), 1)


def moved(tile, shift):
    shift = shift % LANES
    return pltpu.roll(tile, shift, 1) if shift else tile


def cut(get, start, length, last):
    index, offset = divmod(start, LANES)
    tile = moved(get(index), -offset)
    if offset + length <= LANES or index == last:
        return tile
    rest = moved(get(index + 1), LANES - offset)
    return jnp.where(lane_ids(tile.shape[0]) < LANES - offset, tile, rest)


def packed(get, j, segments, length):
    low, high = j * LANES, (j + 1) * LANES
    out = None
    for s in range(segments):
        for i in range(-(-length // LANES)):
            first = s * length + i * LANES
            stop = s * length + min((i + 1) * LANES, length)
            if stop <= low or first >= high:
                continue
            tile = moved(get(s, i), first - low)
            begin = max(first, low) - low
            out = tile if out is None else jnp.where(lane_ids(tile.shape[0]) < begin, out, tile)
    return out


def spread_kernel(v_ref, out_ref, tmp_ref):
    channels, mesh_z, row_count, width = v_ref.shape
    groups, tiles, inner, _ = out_ref.shape
    order = width // 2
    narrow = order // groups
    for t in range(channels):
        for z in range(mesh_z):
            block = v_ref[t, z].astype(jnp.float32)
            zeros = jnp.zeros((LANES - row_count, width), jnp.float32)
            turned = jnp.concatenate([block, zeros], axis=0).T
            for p in range(2):
                for n in range(narrow):
                    start = p * order + n * groups
                    tmp_ref[t * narrow + n, pl.ds(2 * z + p, groups, stride=inner), :] = turned[
                        start : start + groups
                    ]
    for j in range(tiles):
        tile = packed(lambda s, i: tmp_ref[s], j, channels * narrow, row_count)
        out_ref[:, j] = tile.reshape(groups, inner, LANES).astype(jnp.bfloat16)


def whole():
    return pl.BlockSpec(memory_space=pltpu.VMEM)


def spread_rows(vertex, groups):
    channels, mesh_z, row_count, width = vertex.shape
    narrow = width // 2 // groups
    tiles = -(-channels * narrow * row_count // LANES)
    return pl.pallas_call(
        spread_kernel,
        in_specs=[whole()],
        out_specs=whole(),
        out_shape=jax.ShapeDtypeStruct((groups, tiles, 2 * mesh_z, LANES), jnp.bfloat16),
        scratch_shapes=[
            pltpu.VMEM((channels * narrow, groups * 2 * mesh_z, LANES), jnp.float32)
        ],
        compiler_params=pltpu.CompilerParams(vmem_limit_bytes=32 * 1024 * 1024),
    )(vertex)


def transform_kernel(length, x_ref, forward_ref, backward_ref, w_hbm, out_ref, lat_ref, mix_ref, w_ref, sem):
    f32, bf16 = jnp.float32, jnp.bfloat16
    rows = forward_ref.shape[0]
    momenta = rows // 2
    tiles = x_ref.shape[1]
    spans = -(-length // LANES)
    copy = pltpu.make_async_copy(w_hbm, w_ref, sem)
    copy.start()

    def x_tile(j):
        return x_ref[:, j].astype(f32).reshape(rows, LANES)

    pairs = [range(j, min(j + 2, tiles)) for j in range(0, tiles, 2)]
    for pair in pairs:
        x = jnp.concatenate([x_tile(j).astype(bf16) for j in pair], axis=1)
        lattice = jnp.dot(forward_ref[...], x, preferred_element_type=f32).astype(bf16)
        for place, j in enumerate(pair):
            lat_ref[j] = lattice[:, place * LANES : (place + 1) * LANES]
    copy.wait()
    for i in range(spans):
        lanes = pl.ds(i * LANES, LANES)
        for s in range(2):
            part = pl.ds(s * momenta, momenta)
            source = [
                cut(
                    lambda j: lat_ref[j, part].astype(f32),
                    t * length + i * LANES,
                    min(LANES, length - i * LANES),
                    tiles - 1,
                )
                for t in range(3)
            ]
            for t in range(3):
                summed = (
                    w_ref[2 * t, :, lanes] * source[(t + 1) % 3]
                    + w_ref[2 * t + 1, :, lanes] * source[(t + 2) % 3]
                )
                mix_ref[t, i, part] = summed.astype(bf16)
    for pair in pairs:
        mixed = [
            packed(lambda t, i: mix_ref[t, i].astype(f32), j, 3, length).astype(bf16) for j in pair
        ]
        mixed = jnp.concatenate(mixed, axis=1)
        projected = jnp.dot(backward_ref[...], mixed, preferred_element_type=f32).astype(bf16)
        for place, j in enumerate(pair):
            part = projected[:, place * LANES : (place + 1) * LANES].astype(f32)
            out_ref[j] = (x_tile(j) + part).astype(bf16)


def transform(x, forward, backward, w, length):
    groups, tiles, inner, _ = x.shape
    rows = groups * inner
    spans = -(-length // LANES)
    return pl.pallas_call(
        functools.partial(transform_kernel, length),
        in_specs=[whole(), whole(), whole(), pl.BlockSpec(memory_space=pl.ANY)],
        out_specs=whole(),
        out_shape=jax.ShapeDtypeStruct((tiles, rows, LANES), jnp.bfloat16),
        scratch_shapes=[
            pltpu.VMEM((tiles, rows, LANES), jnp.bfloat16),
            pltpu.VMEM((3, spans, rows, LANES), jnp.bfloat16),
            pltpu.VMEM(w.shape, jnp.float32),
            pltpu.SemaphoreType.DMA,
        ],
        compiler_params=pltpu.CompilerParams(vmem_limit_bytes=40 * 1024 * 1024),
    )(x, forward, backward, pltpu.with_memory_space_constraint(w, pltpu.HBM))


def products_kernel(t, narrow, u_ref, loop_ref, out_ref, tall_ref, wide_ref):
    f32, bf16 = jnp.float32, jnp.bfloat16
    tiles, _, cols, groups, _ = u_ref.shape
    order = narrow * groups
    depth = cols * LANES
    row_count = out_ref.shape[1]
    for n in range(narrow):
        for k in range(cols):
            rows, lanes = n * groups, k * LANES
            real, imag = [
                cut(
                    lambda j: u_ref[j, p, k].astype(f32),
                    (t * narrow + n) * row_count,
                    row_count,
                    tiles - 1,
                )
                for p in range(2)
            ]
            minus = (-imag).astype(bf16)
            real, imag = real.astype(bf16), imag.astype(bf16)
            tall_ref[rows : rows + groups, lanes : lanes + LANES] = real
            tall_ref[order + rows : order + rows + groups, lanes : lanes + LANES] = imag
            wide_ref[rows : rows + groups, lanes : lanes + LANES] = real
            wide_ref[rows : rows + groups, depth + lanes : depth + lanes + LANES] = minus
            wide_ref[order + rows : order + rows + groups, lanes : lanes + LANES] = imag
            wide_ref[order + rows : order + rows + groups, depth + lanes : depth + lanes + LANES] = real
    middle = lax.dot_general(
        tall_ref[...], loop_ref[0], (((0,), (0,)), ((), ())), preferred_element_type=f32
    ).astype(bf16)
    change = lax.dot_general(
        middle, wide_ref[...], (((1,), (1,)), ((), ())), preferred_element_type=f32
    )
    increment = (step_length * change).astype(bf16)
    for k in range(cols):
        out_ref[k] = increment[k * LANES : k * LANES + row_count]


def products(t, u, loops, row_count):
    _, _, cols, groups, _ = u.shape
    rows, depth = loops.shape[1:]
    return pl.pallas_call(
        functools.partial(products_kernel, t, rows // 2 // groups),
        grid=(1,),
        in_specs=[whole(), pl.BlockSpec((1, rows, depth), lambda i: (t, 0, 0))],
        out_specs=pl.BlockSpec((cols, row_count, rows), lambda i: (0, 0, 0)),
        out_shape=jax.ShapeDtypeStruct((cols, row_count, rows), jnp.bfloat16),
        scratch_shapes=[
            pltpu.VMEM((rows, depth // 2), jnp.bfloat16),
            pltpu.VMEM((rows, depth), jnp.bfloat16),
        ],
        compiler_params=pltpu.CompilerParams(vmem_limit_bytes=32 * 1024 * 1024),
    )(u, loops)


def per_device(vertex, loop_blocks, mixing, bond_offsets):
    groups = lax.axis_size("pb")
    cols = lax.axis_size("col")
    mesh_z = vertex.shape[1]
    row_count = vertex.shape[2]
    order = vertex.shape[3] // 2
    narrow = order // groups
    momenta = mesh_z * groups
    mesh_y = groups // MX
    sent = spread_rows(vertex, groups)
    gathered = lax.all_to_all(sent, "pb", split_axis=0, concat_axis=0, tiled=True)

    forward, backward = phase_tables(momenta, MX, mesh_y, mesh_z)
    forward = forward.transpose(2, 3, 1, 0).reshape(2 * momenta, 2 * momenta)
    backward = backward.transpose(3, 2, 0, 1).reshape(2 * momenta, 2 * momenta)
    bond = jnp.arange(NB, dtype=jnp.int32)
    own = (jnp.arange(narrow, dtype=jnp.int32) * groups + lax.axis_index("pb")) % NB
    column_bonds = jnp.sum(
        jnp.where((own[:, None] == bond[None, :])[:, :, None], bond_offsets[None], 0), axis=1
    )
    w = shifted_weights(mixing, bond_offsets, column_bonds, row_count, (MX, mesh_y, mesh_z))
    lane_pad = LANES - row_count
    loops = loop_blocks.reshape(3, order, 2, cols, row_count)
    loops = jnp.pad(loops, [(0, 0)] * 4 + [(0, lane_pad)]).reshape(3, order, 2, cols * LANES)
    loop_re, loop_im = loops[:, :, 0], loops[:, :, 1]
    loops = jnp.concatenate(
        [
            jnp.concatenate([loop_re, loop_im], axis=2),
            jnp.concatenate([-loop_im, loop_re], axis=2),
        ],
        axis=1,
    )

    united = transform(gathered, forward, backward, w, narrow * row_count)
    tiles = united.shape[0]
    united = united.reshape(tiles, momenta, 2, LANES).transpose(1, 0, 2, 3)
    sent = lax.all_to_all(united, ("pb", "col"), split_axis=0, concat_axis=0, tiled=True)
    u = sent.reshape(groups, cols, tiles, 2, LANES).transpose(2, 3, 1, 0, 4)
    mine = lax.axis_index("col")
    outs = []
    for t in range(3):
        increment = products(t, u, loops, row_count)
        pieces = []
        for k in range(cols):
            piece = lax.dynamic_index_in_dim(increment, mine ^ k, 0, keepdims=False)
            if k:
                piece = lax.ppermute(piece, "col", [(i, i ^ k) for i in range(cols)])
            pieces.append(piece)
        low, high = (mine & 1) == 1, (mine & 2) == 2
        a, b, c, d = pieces
        a, b = jnp.where(low, b, a), jnp.where(low, a, b)
        c, d = jnp.where(low, d, c), jnp.where(low, c, d)
        a, c = jnp.where(high, c, a), jnp.where(high, a, c)
        b, d = jnp.where(high, d, b), jnp.where(high, b, d)
        returned = jnp.stack([a, b, c, d])
        outs.append(
            (vertex[t].astype(jnp.float32) + returned.astype(jnp.float32)).astype(jnp.bfloat16)
        )
    return jnp.stack(outs)


def solution(mesh):
    return jax.shard_map(
        per_device,
        mesh=mesh,
        in_specs=(P(None, "pb", "col", None), P(None, ("pb", "col"), None, None), P(), P()),
        out_specs=P(None, "pb", "col", None),
        check_vma=False,
    )
```

```python
import functools
import math

import jax
import jax.numpy as jnp
from jax import lax
from jax.experimental import pallas as pl
from jax.experimental.pallas import tpu as pltpu
from jax.sharding import PartitionSpec as P

NB = 7
MX = 8
LANES = 128
PARTS = 4


step_length = 0.25


def mesh_coords(momenta, mesh_y, mesh_z):
    flat_index = jnp.arange(momenta, dtype=jnp.int32)
    coord_x = flat_index // (mesh_y * mesh_z)
    coord_y = flat_index // mesh_z % mesh_y
    coord_z = flat_index % mesh_z
    return (coord_x, coord_y, coord_z)


def phase_tables(momenta, mesh_x, mesh_y, mesh_z):
    coord_x, coord_y, coord_z = mesh_coords(momenta, mesh_y, mesh_z)
    phase_index = (
        coord_x[:, None] * coord_x[None, :] * (mesh_y * mesh_z)
        + coord_y[:, None] * coord_y[None, :] * (mesh_x * mesh_z)
        + coord_z[:, None] * coord_z[None, :] * (mesh_x * mesh_y)
    ) % momenta
    angles = phase_index.astype(jnp.float32) * (2.0 * math.pi / momenta)
    cosine = jnp.cos(angles)
    sine_part = jnp.sin(angles)
    forward = jnp.stack([jnp.stack([cosine, sine_part], 1), jnp.stack([-sine_part, cosine], 1)]) * (
        1.0 / momenta
    )
    backward = jnp.stack([jnp.stack([cosine, -sine_part], 1), jnp.stack([sine_part, cosine], 1)])
    return (forward.astype(jnp.bfloat16), backward.astype(jnp.bfloat16))


def pieces_of(values, axis):
    high = lax.reduce_precision(values, 8, 7)
    rest = values - high
    middle = lax.reduce_precision(rest, 8, 7)
    return jnp.concatenate([high, middle, rest - middle], axis=axis).astype(jnp.bfloat16)


def shifted_slots(bond_offsets, sign, sides):
    mesh_x, mesh_y, mesh_z = sides
    coords = mesh_coords(mesh_x * mesh_y * mesh_z, mesh_y, mesh_z)
    slot = 0
    for axis, side in enumerate(sides):
        moved = jnp.mod(coords[axis][None, :] + sign * bond_offsets[:, axis][:, None], side)
        slot = slot * side + moved
    return slot


def shifted_weights(mixing, bond_offsets, column_bonds, row_count, sides):
    count, momenta = mixing.shape
    f32 = jnp.float32
    slots = shifted_slots(bond_offsets, 1, sides)
    source = lax.broadcasted_iota(jnp.int32, (momenta, NB, momenta), 0)
    picks = (source == slots[None]).astype(jnp.bfloat16).reshape(momenta, NB * momenta)
    first = jnp.dot(pieces_of(mixing, 0), picks, preferred_element_type=f32)
    first = first[:count] + first[count : 2 * count] + first[2 * count :]
    first = first.reshape(count * NB, momenta)
    row = lax.broadcasted_iota(jnp.int32, (count * NB, count * LANES), 0)
    lane = lax.broadcasted_iota(jnp.int32, (count * NB, count * LANES), 1)
    spot = lane % LANES
    spread = (row == lane // LANES * NB + spot % NB) & (spot < row_count)
    spread = spread.astype(jnp.bfloat16)
    wide = jnp.dot(pieces_of(first.T, 0), spread, preferred_element_type=f32)
    wide = wide[:momenta] + wide[momenta : 2 * momenta] + wide[2 * momenta :]
    slots = shifted_slots(column_bonds, -1, sides)
    target = lax.broadcasted_iota(jnp.int32, (NB, momenta, momenta), 2)
    picks = (target == slots[:, :, None]).astype(jnp.bfloat16)
    length = NB * row_count
    spans = -(-length // LANES)
    return pl.pallas_call(
        functools.partial(weights_kernel, row_count),
        in_specs=[whole(), whole()],
        out_specs=whole(),
        out_shape=jax.ShapeDtypeStruct((count, momenta, spans * LANES), f32),
        scratch_shapes=[pltpu.VMEM((NB, count, momenta, LANES), f32)],
        compiler_params=pltpu.CompilerParams(vmem_limit_bytes=32 * 1024 * 1024),
    )(picks, pieces_of(wide, 1))


def weights_kernel(row_count, picks_ref, wide_ref, out_ref, tmp_ref):
    count, momenta, _ = out_ref.shape
    width = count * LANES
    spans = out_ref.shape[2] // LANES

    def pick(n, carry):
        both = jnp.dot(picks_ref[n], wide_ref[...], preferred_element_type=jnp.float32)
        both = both[:, :width] + both[:, width : 2 * width] + both[:, 2 * width :]
        for j in range(count):
            tmp_ref[n, j] = both[:, j * LANES : (j + 1) * LANES]
        return carry

    lax.fori_loop(0, NB, pick, 0)
    edge = NB * row_count - (spans - 1) * LANES

    def pack(j, carry):
        for i in range(spans):
            tile = packed(lambda s, _: tmp_ref[s, j], i, NB, row_count)
            if i == spans - 1:
                tile = jnp.where(lane_ids(momenta) < edge, tile, 0.0)
            out_ref[j, :, i * LANES : (i + 1) * LANES] = tile
        return carry

    lax.fori_loop(0, count, pack, 0)


def lane_ids(rows):
    return lax.broadcasted_iota(jnp.int32, (rows, LANES), 1)


def moved(tile, shift):
    shift = shift % LANES
    return pltpu.roll(tile, shift, 1) if shift else tile


def cut(get, start, length, last):
    index, offset = divmod(start, LANES)
    tile = moved(get(index), -offset)
    if offset + length <= LANES or index == last:
        return tile
    rest = moved(get(index + 1), LANES - offset)
    return jnp.where(lane_ids(tile.shape[0]) < LANES - offset, tile, rest)


def packed(get, j, segments, length):
    low, high = j * LANES, (j + 1) * LANES
    out = None
    for s in range(segments):
        for i in range(-(-length // LANES)):
            first = s * length + i * LANES
            stop = s * length + min((i + 1) * LANES, length)
            if stop <= low or first >= high:
                continue
            tile = moved(get(s, i), first - low)
            begin = max(first, low) - low
            out = tile if out is None else jnp.where(lane_ids(tile.shape[0]) < begin, out, tile)
    return out


def spread_kernel(v_ref, out_ref, tmp_ref):
    channels, mesh_z, row_count, width = v_ref.shape
    groups, tiles, inner, _ = out_ref.shape
    order = width // 2
    narrow = order // groups

    def turn(t, carry):
        for z in range(mesh_z):
            block = v_ref[t, z].astype(jnp.float32)
            zeros = jnp.zeros((LANES - row_count, width), jnp.float32)
            turned = jnp.concatenate([block, zeros], axis=0).T
            for p in range(2):
                for n in range(narrow):
                    start = p * order + n * groups
                    tmp_ref[t * narrow + n, pl.ds(2 * z + p, groups, stride=inner), :] = turned[
                        start : start + groups
                    ]
        return carry

    lax.fori_loop(0, channels, turn, 0)
    share = groups // PARTS

    def pack(c, carry):
        rows = pl.ds(pl.multiple_of(c * share * inner, share * inner), share * inner)
        for j in range(tiles):
            tile = packed(lambda s, _: tmp_ref[s, rows], j, channels * narrow, row_count)
            out_ref[pl.ds(c * share, share), j] = tile.reshape(share, inner, LANES).astype(
                jnp.bfloat16
            )
        return carry

    lax.fori_loop(0, PARTS, pack, 0)


def whole():
    return pl.BlockSpec(memory_space=pltpu.VMEM)


def spread_rows(vertex, groups):
    channels, mesh_z, row_count, width = vertex.shape
    narrow = width // 2 // groups
    tiles = -(-channels * narrow * row_count // LANES)
    return pl.pallas_call(
        spread_kernel,
        in_specs=[whole()],
        out_specs=whole(),
        out_shape=jax.ShapeDtypeStruct((groups, tiles, 2 * mesh_z, LANES), jnp.bfloat16),
        scratch_shapes=[
            pltpu.VMEM((channels * narrow, groups * 2 * mesh_z, LANES), jnp.float32)
        ],
        compiler_params=pltpu.CompilerParams(vmem_limit_bytes=32 * 1024 * 1024),
    )(vertex)


def transform_kernel(
    length, x_ref, forward_ref, backward_ref, w_hbm, out_ref, lat_ref, mix_ref, w_ref, sem
):
    f32, bf16 = jnp.float32, jnp.bfloat16
    rows = forward_ref.shape[0]
    tiles = x_ref.shape[1]
    spans = -(-length // LANES)
    copy = pltpu.make_async_copy(w_hbm, w_ref, sem)
    copy.start()

    def x_tile(j):
        return x_ref[:, j].astype(f32).reshape(rows, LANES)

    def by_pairs(step):
        def pair(i, carry):
            step([2 * i, 2 * i + 1])
            return carry

        lax.fori_loop(0, tiles // 2, pair, 0)
        if tiles % 2:
            step([tiles - 1])

    def forward(places):
        x = jnp.concatenate([x_tile(j).astype(bf16) for j in places], axis=1)
        lattice = jnp.dot(forward_ref[...], x, preferred_element_type=f32).astype(bf16)
        for place, j in enumerate(places):
            lat_ref[j] = lattice[:, place * LANES : (place + 1) * LANES]

    by_pairs(forward)
    copy.wait()
    share = rows // PARTS

    def mix(c, carry):
        part = pl.ds(pl.multiple_of(c * share, share), share)
        half = pl.ds(pl.multiple_of(c % (PARTS // 2) * share, share), share)
        mixed = {}
        for i in range(spans):
            lanes = slice(i * LANES, (i + 1) * LANES)
            source = [
                cut(
                    lambda j: lat_ref[j, part].astype(f32),
                    t * length + i * LANES,
                    min(LANES, length - i * LANES),
                    tiles - 1,
                )
                for t in range(3)
            ]
            for t in range(3):
                summed = (
                    w_ref[2 * t, half, lanes] * source[(t + 1) % 3]
                    + w_ref[2 * t + 1, half, lanes] * source[(t + 2) % 3]
                )
                mixed[t, i] = summed.astype(bf16)
        for j in range(tiles):
            tile = packed(lambda t, i: mixed[t, i].astype(f32), j, 3, length)
            mix_ref[j, part] = tile.astype(bf16)
        return carry

    lax.fori_loop(0, PARTS, mix, 0)

    def backward(places):
        mixed = jnp.concatenate([mix_ref[j] for j in places], axis=1)
        projected = jnp.dot(backward_ref[...], mixed, preferred_element_type=f32).astype(bf16)
        for place, j in enumerate(places):
            part = projected[:, place * LANES : (place + 1) * LANES].astype(f32)
            out_ref[j] = (x_tile(j) + part).astype(bf16)

    by_pairs(backward)


def transform(x, forward, backward, w, length):
    groups, tiles, inner, _ = x.shape
    rows = groups * inner
    return pl.pallas_call(
        functools.partial(transform_kernel, length),
        in_specs=[whole(), whole(), whole(), pl.BlockSpec(memory_space=pl.ANY)],
        out_specs=whole(),
        out_shape=jax.ShapeDtypeStruct((tiles, rows, LANES), jnp.bfloat16),
        scratch_shapes=[
            pltpu.VMEM((tiles, rows, LANES), jnp.bfloat16),
            pltpu.VMEM((tiles, rows, LANES), jnp.bfloat16),
            pltpu.VMEM(w.shape, jnp.float32),
            pltpu.SemaphoreType.DMA,
        ],
        compiler_params=pltpu.CompilerParams(vmem_limit_bytes=40 * 1024 * 1024),
    )(x, forward, backward, pltpu.with_memory_space_constraint(w, pltpu.HBM))


def products_kernel(t, u_ref, loop_hbm, out_ref, loop_ref, tall_ref, wide_ref, sem):
    f32, bf16 = jnp.float32, jnp.bfloat16
    tiles, _, cols, groups, _ = u_ref.shape
    order = tall_ref.shape[0] // 2
    narrow = order // groups
    depth = cols * LANES
    row_count = out_ref.shape[1]
    copy = pltpu.make_async_copy(loop_hbm.at[t], loop_ref, sem)
    copy.start()

    def place(k, carry):
        here = pl.ds(pl.multiple_of(k * LANES, LANES), LANES)
        there = pl.ds(pl.multiple_of(depth + k * LANES, LANES), LANES)
        for n in range(narrow):
            real, imag = [
                cut(
                    lambda j: u_ref[j, p, k].astype(f32),
                    (t * narrow + n) * row_count,
                    row_count,
                    tiles - 1,
                )
                for p in range(2)
            ]
            minus = (-imag).astype(bf16)
            real, imag = real.astype(bf16), imag.astype(bf16)
            upper = slice(n * groups, (n + 1) * groups)
            lower = slice(order + n * groups, order + (n + 1) * groups)
            tall_ref[upper, here] = real
            tall_ref[lower, here] = imag
            wide_ref[upper, here] = real
            wide_ref[upper, there] = minus
            wide_ref[lower, here] = imag
            wide_ref[lower, there] = real
        return carry

    lax.fori_loop(0, cols, place, 0)
    copy.wait()
    middle = lax.dot_general(
        tall_ref[...], loop_ref[...], (((0,), (0,)), ((), ())), preferred_element_type=f32
    ).astype(bf16)
    change = lax.dot_general(
        middle, wide_ref[...], (((1,), (1,)), ((), ())), preferred_element_type=f32
    )
    increment = (step_length * change).astype(bf16)
    for k in range(cols):
        out_ref[k] = increment[k * LANES : k * LANES + row_count]


def products(t, u, loops, row_count):
    cols = u.shape[2]
    rows, depth = loops.shape[1:]
    return pl.pallas_call(
        functools.partial(products_kernel, t),
        in_specs=[whole(), pl.BlockSpec(memory_space=pl.ANY)],
        out_specs=whole(),
        out_shape=jax.ShapeDtypeStruct((cols, row_count, rows), jnp.bfloat16),
        scratch_shapes=[
            pltpu.VMEM((rows, depth), jnp.bfloat16),
            pltpu.VMEM((rows, depth // 2), jnp.bfloat16),
            pltpu.VMEM((rows, depth), jnp.bfloat16),
            pltpu.SemaphoreType.DMA,
        ],
        compiler_params=pltpu.CompilerParams(vmem_limit_bytes=32 * 1024 * 1024),
    )(u, pltpu.with_memory_space_constraint(loops, pltpu.HBM))


def per_device(vertex, loop_blocks, mixing, bond_offsets):
    groups = lax.axis_size("pb")
    cols = lax.axis_size("col")
    mesh_z = vertex.shape[1]
    row_count = vertex.shape[2]
    order = vertex.shape[3] // 2
    narrow = order // groups
    momenta = mesh_z * groups
    mesh_y = groups // MX
    sent = spread_rows(vertex, groups)
    gathered = lax.all_to_all(sent, "pb", split_axis=0, concat_axis=0, tiled=True)

    forward, backward = phase_tables(momenta, MX, mesh_y, mesh_z)
    forward = forward.transpose(2, 3, 1, 0).reshape(2 * momenta, 2 * momenta)
    backward = backward.transpose(3, 2, 0, 1).reshape(2 * momenta, 2 * momenta)
    bond = jnp.arange(NB, dtype=jnp.int32)
    own = (jnp.arange(narrow, dtype=jnp.int32) * groups + lax.axis_index("pb")) % NB
    column_bonds = jnp.sum(
        jnp.where((own[:, None] == bond[None, :])[:, :, None], bond_offsets[None], 0), axis=1
    )
    w = shifted_weights(mixing, bond_offsets, column_bonds, row_count, (MX, mesh_y, mesh_z))
    lane_pad = LANES - row_count
    loops = loop_blocks.reshape(3, order, 2, cols, row_count)
    loops = jnp.pad(loops, [(0, 0)] * 4 + [(0, lane_pad)]).reshape(3, order, 2, cols * LANES)
    loop_re, loop_im = loops[:, :, 0], loops[:, :, 1]
    loops = jnp.concatenate(
        [
            jnp.concatenate([loop_re, loop_im], axis=2),
            jnp.concatenate([-loop_im, loop_re], axis=2),
        ],
        axis=1,
    )

    united = transform(gathered, forward, backward, w, narrow * row_count)
    tiles = united.shape[0]
    united = united.reshape(tiles, momenta, 2, LANES).transpose(1, 0, 2, 3)
    sent = lax.all_to_all(united, ("pb", "col"), split_axis=0, concat_axis=0, tiled=True)
    u = sent.reshape(groups, cols, tiles, 2, LANES).transpose(2, 3, 1, 0, 4)
    mine = lax.axis_index("col")
    parts = []
    for t in range(3):
        if t:
            u, parts[-1][1] = lax.optimization_barrier((u, parts[-1][1]))
        increment = products(t, u, loops, row_count)
        pieces = []
        for k in range(cols):
            piece = lax.dynamic_index_in_dim(increment, mine ^ k, 0, keepdims=False)
            if k:
                piece = lax.ppermute(piece, "col", [(i, i ^ k) for i in range(cols)])
            pieces.append(piece)
        parts.append(pieces)
    outs = []
    for t in range(3):
        low, high = (mine & 1) == 1, (mine & 2) == 2
        a, b, c, d = parts[t]
        a, b = jnp.where(low, b, a), jnp.where(low, a, b)
        c, d = jnp.where(low, d, c), jnp.where(low, c, d)
        a, c = jnp.where(high, c, a), jnp.where(high, a, c)
        b, d = jnp.where(high, d, b), jnp.where(high, b, d)
        returned = jnp.stack([a, b, c, d])
        outs.append(
            (vertex[t].astype(jnp.float32) + returned.astype(jnp.float32)).astype(jnp.bfloat16)
        )
    return jnp.stack(outs)


def solution(mesh):
    return jax.shard_map(
        per_device,
        mesh=mesh,
        in_specs=(P(None, "pb", "col", None), P(None, ("pb", "col"), None, None), P(), P()),
        out_specs=P(None, "pb", "col", None),
        check_vma=False,
    )
```

```python
import functools
import math

import jax
import jax.numpy as jnp
from jax import lax
from jax.experimental import pallas as pl
from jax.experimental.pallas import tpu as pltpu
from jax.sharding import PartitionSpec as P

NB = 7
MX = 8
LANES = 128
PARTS = 4


step_length = 0.25


def mesh_coords(momenta, mesh_y, mesh_z):
    flat_index = jnp.arange(momenta, dtype=jnp.int32)
    coord_x = flat_index // (mesh_y * mesh_z)
    coord_y = flat_index // mesh_z % mesh_y
    coord_z = flat_index % mesh_z
    return (coord_x, coord_y, coord_z)


def phase_tables(momenta, mesh_x, mesh_y, mesh_z):
    coord_x, coord_y, coord_z = mesh_coords(momenta, mesh_y, mesh_z)
    phase_index = (
        coord_x[:, None] * coord_x[None, :] * (mesh_y * mesh_z)
        + coord_y[:, None] * coord_y[None, :] * (mesh_x * mesh_z)
        + coord_z[:, None] * coord_z[None, :] * (mesh_x * mesh_y)
    ) % momenta
    angles = phase_index.astype(jnp.float32) * (2.0 * math.pi / momenta)
    cosine = jnp.cos(angles)
    sine_part = jnp.sin(angles)
    forward = jnp.stack([jnp.stack([cosine, sine_part], 1), jnp.stack([-sine_part, cosine], 1)]) * (
        1.0 / momenta
    )
    backward = jnp.stack([jnp.stack([cosine, -sine_part], 1), jnp.stack([sine_part, cosine], 1)])
    return (forward.astype(jnp.bfloat16), backward.astype(jnp.bfloat16))


def pieces_of(values, axis):
    high = lax.reduce_precision(values, 8, 7)
    rest = values - high
    middle = lax.reduce_precision(rest, 8, 7)
    return jnp.concatenate([high, middle, rest - middle], axis=axis).astype(jnp.bfloat16)


def shifted_slots(bond_offsets, sign, sides):
    mesh_x, mesh_y, mesh_z = sides
    coords = mesh_coords(mesh_x * mesh_y * mesh_z, mesh_y, mesh_z)
    slot = 0
    for axis, side in enumerate(sides):
        moved = jnp.mod(coords[axis][None, :] + sign * bond_offsets[:, axis][:, None], side)
        slot = slot * side + moved
    return slot


def shifted_weights(mixing, bond_offsets, column_bonds, row_count, sides):
    count, momenta = mixing.shape
    f32 = jnp.float32
    slots = shifted_slots(bond_offsets, 1, sides)
    source = lax.broadcasted_iota(jnp.int32, (momenta, NB, momenta), 0)
    picks = (source == slots[None]).astype(jnp.bfloat16).reshape(momenta, NB * momenta)
    first = jnp.dot(pieces_of(mixing, 0), picks, preferred_element_type=f32)
    first = first[:count] + first[count : 2 * count] + first[2 * count :]
    first = first.reshape(count * NB, momenta)
    row = lax.broadcasted_iota(jnp.int32, (count * NB, count * LANES), 0)
    lane = lax.broadcasted_iota(jnp.int32, (count * NB, count * LANES), 1)
    spot = lane % LANES
    spread = (row == lane // LANES * NB + spot % NB) & (spot < row_count)
    spread = spread.astype(jnp.bfloat16)
    wide = jnp.dot(pieces_of(first.T, 0), spread, preferred_element_type=f32)
    wide = wide[:momenta] + wide[momenta : 2 * momenta] + wide[2 * momenta :]
    slots = shifted_slots(column_bonds, -1, sides)
    target = lax.broadcasted_iota(jnp.int32, (NB, momenta, momenta), 2)
    picks = (target == slots[:, :, None]).astype(jnp.bfloat16)
    length = NB * row_count
    spans = -(-length // LANES)
    return pl.pallas_call(
        functools.partial(weights_kernel, row_count),
        in_specs=[whole(), whole()],
        out_specs=whole(),
        out_shape=jax.ShapeDtypeStruct((count, momenta, spans * LANES), f32),
        scratch_shapes=[pltpu.VMEM((NB, count, momenta, LANES), f32)],
        compiler_params=pltpu.CompilerParams(vmem_limit_bytes=32 * 1024 * 1024),
    )(picks, pieces_of(wide, 1))


def weights_kernel(row_count, picks_ref, wide_ref, out_ref, tmp_ref):
    count, momenta, _ = out_ref.shape
    width = count * LANES
    spans = out_ref.shape[2] // LANES

    def pick(n, carry):
        both = jnp.dot(picks_ref[n], wide_ref[...], preferred_element_type=jnp.float32)
        both = both[:, :width] + both[:, width : 2 * width] + both[:, 2 * width :]
        for j in range(count):
            tmp_ref[n, j] = both[:, j * LANES : (j + 1) * LANES]
        return carry

    lax.fori_loop(0, NB, pick, 0)
    edge = NB * row_count - (spans - 1) * LANES

    def pack(j, carry):
        for i in range(spans):
            tile = packed(lambda s, _: tmp_ref[s, j], i, NB, row_count)
            if i == spans - 1:
                tile = jnp.where(lane_ids(momenta) < edge, tile, 0.0)
            out_ref[j, :, i * LANES : (i + 1) * LANES] = tile
        return carry

    lax.fori_loop(0, count, pack, 0)


def lane_ids(rows):
    return lax.broadcasted_iota(jnp.int32, (rows, LANES), 1)


def moved(tile, shift):
    shift = shift % LANES
    return pltpu.roll(tile, shift, 1) if shift else tile


def cut(get, start, length, last):
    index, offset = divmod(start, LANES)
    tile = moved(get(index), -offset)
    if offset + length <= LANES or index == last:
        return tile
    rest = moved(get(index + 1), LANES - offset)
    return jnp.where(lane_ids(tile.shape[0]) < LANES - offset, tile, rest)


def packed(get, j, segments, length):
    low, high = j * LANES, (j + 1) * LANES
    out = None
    for s in range(segments):
        for i in range(-(-length // LANES)):
            first = s * length + i * LANES
            stop = s * length + min((i + 1) * LANES, length)
            if stop <= low or first >= high:
                continue
            tile = moved(get(s, i), first - low)
            begin = max(first, low) - low
            out = tile if out is None else jnp.where(lane_ids(tile.shape[0]) < begin, out, tile)
    return out


def spread_kernel(v_hbm, out_hbm, v_ref, tmp_ref, out_ref, in_sems, out_sems):
    channels, mesh_z, row_count, width = v_ref.shape
    groups, tiles, inner, _ = out_ref.shape
    order = width // 2
    narrow = order // groups
    share = groups // PARTS
    arriving = [
        pltpu.make_async_copy(v_hbm.at[t], v_ref.at[t], in_sems.at[t]) for t in range(channels)
    ]
    for copy in arriving:
        copy.start()

    for t in range(channels):
        arriving[t].wait()

        def turn(z, carry):
            block = v_ref[t, z].astype(jnp.float32)
            zeros = jnp.zeros((LANES - row_count, width), jnp.float32)
            turned = jnp.concatenate([block, zeros], axis=0).T
            for p in range(2):
                for n in range(narrow):
                    start = p * order + n * groups
                    tmp_ref[t * narrow + n, pl.ds(2 * z + p, groups, stride=inner), :] = turned[
                        start : start + groups
                    ]
            return carry

        lax.fori_loop(0, mesh_z, turn, 0)

    leaving = []
    for c in range(PARTS):
        part = pl.ds(c * share, share)
        leaving.append(pltpu.make_async_copy(out_ref.at[part], out_hbm.at[part], out_sems.at[c]))
        rows = pl.ds(c * share * inner, share * inner)
        for j in range(tiles):
            tile = packed(lambda s, i: tmp_ref[s, rows], j, channels * narrow, row_count)
            out_ref[part, j] = tile.reshape(share, inner, LANES).astype(jnp.bfloat16)
        leaving[c].start()
    for copy in leaving:
        copy.wait()


def whole():
    return pl.BlockSpec(memory_space=pltpu.VMEM)


def spread_rows(vertex, groups):
    channels, mesh_z, row_count, width = vertex.shape
    narrow = width // 2 // groups
    tiles = -(-channels * narrow * row_count // LANES)
    shape = (groups, tiles, 2 * mesh_z, LANES)
    return pl.pallas_call(
        spread_kernel,
        in_specs=[pl.BlockSpec(memory_space=pltpu.HBM)],
        out_specs=pl.BlockSpec(memory_space=pltpu.HBM),
        out_shape=pltpu.HBM(shape, jnp.bfloat16),
        scratch_shapes=[
            pltpu.VMEM(vertex.shape, jnp.bfloat16),
            pltpu.VMEM((channels * narrow, groups * 2 * mesh_z, LANES), jnp.float32),
            pltpu.VMEM(shape, jnp.bfloat16),
            pltpu.SemaphoreType.DMA((channels,)),
            pltpu.SemaphoreType.DMA((PARTS,)),
        ],
        compiler_params=pltpu.CompilerParams(vmem_limit_bytes=32 * 1024 * 1024),
    )(pltpu.with_memory_space_constraint(vertex, pltpu.HBM))


def transform_kernel(
    length, x_ref, forward_ref, backward_ref, w_hbm, out_ref, lat_ref, mix_ref, w_ref, sem
):
    f32, bf16 = jnp.float32, jnp.bfloat16
    rows = forward_ref.shape[0]
    tiles = x_ref.shape[1]
    spans = -(-length // LANES)
    copy = pltpu.make_async_copy(w_hbm, w_ref, sem)
    copy.start()

    def x_tile(j):
        return x_ref[:, j].astype(f32).reshape(rows, LANES)

    def by_pairs(step):
        def pair(i, carry):
            step([2 * i, 2 * i + 1])
            return carry

        lax.fori_loop(0, tiles // 2, pair, 0)
        if tiles % 2:
            step([tiles - 1])

    def forward(places):
        x = jnp.concatenate([x_tile(j).astype(bf16) for j in places], axis=1)
        lattice = jnp.dot(forward_ref[...], x, preferred_element_type=f32).astype(bf16)
        for place, j in enumerate(places):
            lat_ref[j] = lattice[:, place * LANES : (place + 1) * LANES]

    by_pairs(forward)
    copy.wait()
    share = rows // PARTS

    def mix(c, carry):
        part = pl.ds(pl.multiple_of(c * share, share), share)
        half = pl.ds(pl.multiple_of(c % (PARTS // 2) * share, share), share)
        mixed = {}
        for i in range(spans):
            lanes = slice(i * LANES, (i + 1) * LANES)
            source = [
                cut(
                    lambda j: lat_ref[j, part].astype(f32),
                    t * length + i * LANES,
                    min(LANES, length - i * LANES),
                    tiles - 1,
                )
                for t in range(3)
            ]
            for t in range(3):
                summed = (
                    w_ref[2 * t, half, lanes] * source[(t + 1) % 3]
                    + w_ref[2 * t + 1, half, lanes] * source[(t + 2) % 3]
                )
                mixed[t, i] = summed.astype(bf16)
        for j in range(tiles):
            tile = packed(lambda t, i: mixed[t, i].astype(f32), j, 3, length)
            mix_ref[j, part] = tile.astype(bf16)
        return carry

    lax.fori_loop(0, PARTS, mix, 0)

    def backward(places):
        mixed = jnp.concatenate([mix_ref[j] for j in places], axis=1)
        projected = jnp.dot(backward_ref[...], mixed, preferred_element_type=f32).astype(bf16)
        for place, j in enumerate(places):
            part = projected[:, place * LANES : (place + 1) * LANES].astype(f32)
            out_ref[j] = (x_tile(j) + part).astype(bf16)

    by_pairs(backward)


def transform(x, forward, backward, w, length):
    groups, tiles, inner, _ = x.shape
    rows = groups * inner
    return pl.pallas_call(
        functools.partial(transform_kernel, length),
        in_specs=[whole(), whole(), whole(), pl.BlockSpec(memory_space=pl.ANY)],
        out_specs=whole(),
        out_shape=jax.ShapeDtypeStruct((tiles, rows, LANES), jnp.bfloat16),
        scratch_shapes=[
            pltpu.VMEM((tiles, rows, LANES), jnp.bfloat16),
            pltpu.VMEM((tiles, rows, LANES), jnp.bfloat16),
            pltpu.VMEM(w.shape, jnp.float32),
            pltpu.SemaphoreType.DMA,
        ],
        compiler_params=pltpu.CompilerParams(vmem_limit_bytes=40 * 1024 * 1024),
    )(x, forward, backward, pltpu.with_memory_space_constraint(w, pltpu.HBM))


def products_kernel(t, mine_ref, u_ref, loop_hbm, *refs):
    out_refs, (loop_ref, tall_ref, wide_ref, sem) = refs[:-4], refs[-4:]
    f32, bf16 = jnp.float32, jnp.bfloat16
    mine = mine_ref[0]
    tiles, _, cols, groups, _ = u_ref.shape
    order = tall_ref.shape[0] // 2
    narrow = order // groups
    depth = cols * LANES
    row_count = out_refs[0].shape[0]
    copy = pltpu.make_async_copy(loop_hbm.at[t], loop_ref, sem)
    copy.start()

    def place(k, carry):
        here = pl.ds(pl.multiple_of(k * LANES, LANES), LANES)
        slab = pl.ds(pl.multiple_of((k ^ mine) * LANES, LANES), LANES)
        there = pl.ds(pl.multiple_of(depth + k * LANES, LANES), LANES)
        for n in range(narrow):
            real, imag = [
                cut(
                    lambda j: u_ref[j, p, k].astype(f32),
                    (t * narrow + n) * row_count,
                    row_count,
                    tiles - 1,
                )
                for p in range(2)
            ]
            minus = (-imag).astype(bf16)
            real, imag = real.astype(bf16), imag.astype(bf16)
            upper = slice(n * groups, (n + 1) * groups)
            lower = slice(order + n * groups, order + (n + 1) * groups)
            tall_ref[upper, slab] = real
            tall_ref[lower, slab] = imag
            wide_ref[upper, here] = real
            wide_ref[upper, there] = minus
            wide_ref[lower, here] = imag
            wide_ref[lower, there] = real
        return carry

    lax.fori_loop(0, cols, place, 0)
    copy.wait()
    middle = lax.dot_general(
        tall_ref[...], loop_ref[...], (((0,), (0,)), ((), ())), preferred_element_type=f32
    ).astype(bf16)
    change = lax.dot_general(
        middle, wide_ref[...], (((1,), (1,)), ((), ())), preferred_element_type=f32
    )
    increment = (step_length * change).astype(bf16)
    for k in range(cols):
        out_refs[k][...] = increment[k * LANES : k * LANES + row_count]


def products(t, mine, u, loops, row_count):
    cols = u.shape[2]
    rows, depth = loops.shape[1:]
    return pl.pallas_call(
        functools.partial(products_kernel, t),
        in_specs=[
            pl.BlockSpec(memory_space=pltpu.SMEM),
            whole(),
            pl.BlockSpec(memory_space=pl.ANY),
        ],
        out_specs=[whole()] * cols,
        out_shape=[jax.ShapeDtypeStruct((row_count, rows), jnp.bfloat16)] * cols,
        scratch_shapes=[
            pltpu.VMEM((rows, depth), jnp.bfloat16),
            pltpu.VMEM((rows, depth // 2), jnp.bfloat16),
            pltpu.VMEM((rows, depth), jnp.bfloat16),
            pltpu.SemaphoreType.DMA,
        ],
        compiler_params=pltpu.CompilerParams(vmem_limit_bytes=32 * 1024 * 1024),
    )(mine, u, pltpu.with_memory_space_constraint(loops, pltpu.HBM))


def finish_kernel(t, count, mine_ref, v_ref, *refs):
    piece_refs, out_hbm, (new_ref, sems) = refs[:count], refs[-3], refs[-2:]
    mine = mine_ref[0]
    copies = []
    for k in range(count):
        q = mine ^ k
        total = v_ref[0, q].astype(jnp.float32) + piece_refs[k][...].astype(jnp.float32)
        new_ref[k] = total.astype(jnp.bfloat16)
        copies.append(pltpu.make_async_copy(new_ref.at[k], out_hbm.at[t, q], sems.at[k]))
        copies[k].start()
    for copy in copies:
        copy.wait()


def finish(t, mine, vertex, pieces, out):
    count = len(pieces)
    operands = [mine, vertex, *pieces]
    specs = [
        pl.BlockSpec(memory_space=pltpu.SMEM),
        pl.BlockSpec((1,) + vertex.shape[1:], lambda i: (t, 0, 0, 0)),
    ] + [whole()] * count
    aliases = {}
    if out is not None:
        aliases = {len(operands): 0}
        operands.append(out)
        specs.append(pl.BlockSpec(memory_space=pltpu.HBM))
    return pl.pallas_call(
        functools.partial(finish_kernel, t, count),
        grid=(1,),
        in_specs=specs,
        out_specs=pl.BlockSpec(memory_space=pltpu.HBM),
        out_shape=jax.ShapeDtypeStruct(vertex.shape, vertex.dtype),
        input_output_aliases=aliases,
        scratch_shapes=[
            pltpu.VMEM((count,) + vertex.shape[2:], vertex.dtype),
            pltpu.SemaphoreType.DMA((count,)),
        ],
        compiler_params=pltpu.CompilerParams(vmem_limit_bytes=16 * 1024 * 1024),
    )(*operands)


def per_device(vertex, loop_blocks, mixing, bond_offsets):
    groups = lax.axis_size("pb")
    cols = lax.axis_size("col")
    mesh_z = vertex.shape[1]
    row_count = vertex.shape[2]
    order = vertex.shape[3] // 2
    narrow = order // groups
    momenta = mesh_z * groups
    mesh_y = groups // MX
    sent = spread_rows(vertex, groups)
    gathered = lax.all_to_all(sent, "pb", split_axis=0, concat_axis=0, tiled=True)

    forward, backward = phase_tables(momenta, MX, mesh_y, mesh_z)
    forward = forward.transpose(2, 3, 1, 0).reshape(2 * momenta, 2 * momenta)
    backward = backward.transpose(3, 2, 0, 1).reshape(2 * momenta, 2 * momenta)
    bond = jnp.arange(NB, dtype=jnp.int32)
    own = (jnp.arange(narrow, dtype=jnp.int32) * groups + lax.axis_index("pb")) % NB
    column_bonds = jnp.sum(
        jnp.where((own[:, None] == bond[None, :])[:, :, None], bond_offsets[None], 0), axis=1
    )
    w = shifted_weights(mixing, bond_offsets, column_bonds, row_count, (MX, mesh_y, mesh_z))
    lane_pad = LANES - row_count
    loops = loop_blocks.reshape(3, order, 2, cols, row_count)
    loops = jnp.pad(loops, [(0, 0)] * 4 + [(0, lane_pad)]).reshape(3, order, 2, cols * LANES)
    loop_re, loop_im = loops[:, :, 0], loops[:, :, 1]
    loops = jnp.concatenate(
        [
            jnp.concatenate([loop_re, loop_im], axis=2),
            jnp.concatenate([-loop_im, loop_re], axis=2),
        ],
        axis=1,
    )

    united = transform(gathered, forward, backward, w, narrow * row_count)
    tiles = united.shape[0]
    united = united.reshape(tiles, momenta, 2, LANES).transpose(1, 0, 2, 3)
    sent = lax.all_to_all(united, ("pb", "col"), split_axis=0, concat_axis=0, tiled=True)
    u = sent.reshape(groups, cols, tiles, 2, LANES).transpose(2, 3, 1, 0, 4)
    mine = lax.axis_index("col").astype(jnp.int32).reshape(1)
    parts = []
    for t in range(3):
        if t:
            u, parts[0][1] = lax.optimization_barrier((u, parts[0][1]))
        pieces = list(products(t, mine, u, loops, row_count))
        for k in reversed(range(1, cols)):
            pieces[k] = lax.ppermute(pieces[k], "col", [(i, i ^ k) for i in range(cols)])
        parts.append(pieces)
    out = None
    for t in range(3):
        out = finish(t, mine, vertex, parts[t], out)
    return out


def solution(mesh):
    return jax.shard_map(
        per_device,
        mesh=mesh,
        in_specs=(P(None, "pb", "col", None), P(None, ("pb", "col"), None, None), P(), P()),
        out_specs=P(None, "pb", "col", None),
        check_vma=False,
    )
```

```python
import functools
import math

import jax
import jax.numpy as jnp
from jax import lax
from jax.experimental import pallas as pl
from jax.experimental.pallas import tpu as pltpu
from jax.sharding import PartitionSpec as P

NB = 7
MX = 8
LANES = 128
PARTS = 4


step_length = 0.25


def mesh_coords(momenta, mesh_y, mesh_z):
    flat_index = jnp.arange(momenta, dtype=jnp.int32)
    coord_x = flat_index // (mesh_y * mesh_z)
    coord_y = flat_index // mesh_z % mesh_y
    coord_z = flat_index % mesh_z
    return (coord_x, coord_y, coord_z)


def phase_tables(momenta, mesh_x, mesh_y, mesh_z):
    coord_x, coord_y, coord_z = mesh_coords(momenta, mesh_y, mesh_z)
    phase_index = (
        coord_x[:, None] * coord_x[None, :] * (mesh_y * mesh_z)
        + coord_y[:, None] * coord_y[None, :] * (mesh_x * mesh_z)
        + coord_z[:, None] * coord_z[None, :] * (mesh_x * mesh_y)
    ) % momenta
    angles = phase_index.astype(jnp.float32) * (2.0 * math.pi / momenta)
    cosine = jnp.cos(angles)
    sine_part = jnp.sin(angles)
    forward = jnp.stack([jnp.stack([cosine, sine_part], 1), jnp.stack([-sine_part, cosine], 1)]) * (
        1.0 / momenta
    )
    backward = jnp.stack([jnp.stack([cosine, -sine_part], 1), jnp.stack([sine_part, cosine], 1)])
    return (forward.astype(jnp.bfloat16), backward.astype(jnp.bfloat16))


def pieces_of(values, axis):
    high = lax.reduce_precision(values, 8, 7)
    rest = values - high
    middle = lax.reduce_precision(rest, 8, 7)
    return jnp.concatenate([high, middle, rest - middle], axis=axis).astype(jnp.bfloat16)


def shifted_slots(bond_offsets, sign, sides):
    mesh_x, mesh_y, mesh_z = sides
    coords = mesh_coords(mesh_x * mesh_y * mesh_z, mesh_y, mesh_z)
    slot = 0
    for axis, side in enumerate(sides):
        moved = jnp.mod(coords[axis][None, :] + sign * bond_offsets[:, axis][:, None], side)
        slot = slot * side + moved
    return slot


def shifted_weights(mixing, bond_offsets, column_bonds, row_count, sides):
    count, momenta = mixing.shape
    f32 = jnp.float32
    slots = shifted_slots(bond_offsets, 1, sides)
    source = lax.broadcasted_iota(jnp.int32, (momenta, NB, momenta), 0)
    picks = (source == slots[None]).astype(jnp.bfloat16).reshape(momenta, NB * momenta)
    first = jnp.dot(pieces_of(mixing, 0), picks, preferred_element_type=f32)
    first = first[:count] + first[count : 2 * count] + first[2 * count :]
    first = first.reshape(count * NB, momenta)
    row = lax.broadcasted_iota(jnp.int32, (count * NB, count * LANES), 0)
    lane = lax.broadcasted_iota(jnp.int32, (count * NB, count * LANES), 1)
    spot = lane % LANES
    spread = (row == lane // LANES * NB + spot % NB) & (spot < row_count)
    spread = spread.astype(jnp.bfloat16)
    wide = jnp.dot(pieces_of(first.T, 0), spread, preferred_element_type=f32)
    wide = wide[:momenta] + wide[momenta : 2 * momenta] + wide[2 * momenta :]
    slots = shifted_slots(column_bonds, -1, sides)
    target = lax.broadcasted_iota(jnp.int32, (NB, momenta, momenta), 2)
    picks = (target == slots[:, :, None]).astype(jnp.bfloat16)
    length = NB * row_count
    spans = -(-length // LANES)
    return pl.pallas_call(
        functools.partial(weights_kernel, row_count),
        in_specs=[whole(), whole()],
        out_specs=whole(),
        out_shape=jax.ShapeDtypeStruct((count, momenta, spans * LANES), f32),
        scratch_shapes=[pltpu.VMEM((NB, count, momenta, LANES), f32)],
        compiler_params=pltpu.CompilerParams(vmem_limit_bytes=32 * 1024 * 1024),
    )(picks, pieces_of(wide, 1))


def weights_kernel(row_count, picks_ref, wide_ref, out_ref, tmp_ref):
    count, momenta, _ = out_ref.shape
    width = count * LANES
    spans = out_ref.shape[2] // LANES

    def pick(n, carry):
        both = jnp.dot(picks_ref[n], wide_ref[...], preferred_element_type=jnp.float32)
        both = both[:, :width] + both[:, width : 2 * width] + both[:, 2 * width :]
        for j in range(count):
            tmp_ref[n, j] = both[:, j * LANES : (j + 1) * LANES]
        return carry

    lax.fori_loop(0, NB, pick, 0)
    edge = NB * row_count - (spans - 1) * LANES

    def pack(j, carry):
        for i in range(spans):
            tile = packed(lambda s, _: tmp_ref[s, j], i, NB, row_count)
            if i == spans - 1:
                tile = jnp.where(lane_ids(momenta) < edge, tile, 0.0)
            out_ref[j, :, i * LANES : (i + 1) * LANES] = tile
        return carry

    lax.fori_loop(0, count, pack, 0)


def lane_ids(rows):
    return lax.broadcasted_iota(jnp.int32, (rows, LANES), 1)


def moved(tile, shift):
    shift = shift % LANES
    return pltpu.roll(tile, shift, 1) if shift else tile


def cut(get, start, length, last):
    index, offset = divmod(start, LANES)
    tile = moved(get(index), -offset)
    if offset + length <= LANES or index == last:
        return tile
    rest = moved(get(index + 1), LANES - offset)
    return jnp.where(lane_ids(tile.shape[0]) < LANES - offset, tile, rest)


def packed(get, j, segments, length):
    low, high = j * LANES, (j + 1) * LANES
    out = None
    for s in range(segments):
        for i in range(-(-length // LANES)):
            first = s * length + i * LANES
            stop = s * length + min((i + 1) * LANES, length)
            if stop <= low or first >= high:
                continue
            tile = moved(get(s, i), first - low)
            begin = max(first, low) - low
            out = tile if out is None else jnp.where(lane_ids(tile.shape[0]) < begin, out, tile)
    return out


def spread_kernel(v_hbm, out_hbm, v_ref, tmp_ref, out_ref, in_sems, out_sems):
    channels, mesh_z, row_count, width = v_ref.shape
    groups, tiles, inner, _ = out_ref.shape
    order = width // 2
    narrow = order // groups
    share = groups // PARTS
    arriving = [
        pltpu.make_async_copy(v_hbm.at[t], v_ref.at[t], in_sems.at[t]) for t in range(channels)
    ]
    for copy in arriving:
        copy.start()

    for t in range(channels):
        arriving[t].wait()

        for z in range(mesh_z):
            block = v_ref[t, z].astype(jnp.float32)
            zeros = jnp.zeros((LANES - row_count, width), jnp.float32)
            turned = jnp.concatenate([block, zeros], axis=0).T
            for p in range(2):
                for n in range(narrow):
                    start = p * order + n * groups
                    tmp_ref[t * narrow + n, pl.ds(2 * z + p, groups, stride=inner), :] = turned[
                        start : start + groups
                    ]

    leaving = []
    for c in range(PARTS):
        part = pl.ds(c * share, share)
        leaving.append(pltpu.make_async_copy(out_ref.at[part], out_hbm.at[part], out_sems.at[c]))
        rows = pl.ds(c * share * inner, share * inner)
        for j in range(tiles):
            tile = packed(lambda s, i: tmp_ref[s, rows], j, channels * narrow, row_count)
            out_ref[part, j] = tile.reshape(share, inner, LANES).astype(jnp.bfloat16)
        leaving[c].start()
    for copy in leaving:
        copy.wait()


def whole():
    return pl.BlockSpec(memory_space=pltpu.VMEM)


def spread_rows(vertex, groups):
    channels, mesh_z, row_count, width = vertex.shape
    narrow = width // 2 // groups
    tiles = -(-channels * narrow * row_count // LANES)
    shape = (groups, tiles, 2 * mesh_z, LANES)
    return pl.pallas_call(
        spread_kernel,
        in_specs=[pl.BlockSpec(memory_space=pltpu.HBM)],
        out_specs=pl.BlockSpec(memory_space=pltpu.HBM),
        out_shape=pltpu.HBM(shape, jnp.bfloat16),
        scratch_shapes=[
            pltpu.VMEM(vertex.shape, jnp.bfloat16),
            pltpu.VMEM((channels * narrow, groups * 2 * mesh_z, LANES), jnp.float32),
            pltpu.VMEM(shape, jnp.bfloat16),
            pltpu.SemaphoreType.DMA((channels,)),
            pltpu.SemaphoreType.DMA((PARTS,)),
        ],
        compiler_params=pltpu.CompilerParams(vmem_limit_bytes=32 * 1024 * 1024),
    )(pltpu.with_memory_space_constraint(vertex, pltpu.HBM))


def transform_kernel(
    length, x_ref, forward_ref, backward_ref, w_hbm, out_ref, lat_ref, mix_ref, turn_ref, w_ref, sem
):
    f32, bf16 = jnp.float32, jnp.bfloat16
    rows = forward_ref.shape[0]
    momenta = rows // 2
    tiles = x_ref.shape[1]
    spans = -(-length // LANES)
    copy = pltpu.make_async_copy(w_hbm, w_ref, sem)
    copy.start()

    def x_tile(j):
        return x_ref[:, j].astype(f32).reshape(rows, LANES)

    def by_pairs(step):
        def pair(i, carry):
            step([2 * i, 2 * i + 1])
            return carry

        lax.fori_loop(0, tiles // 2, pair, 0, unroll=3)
        if tiles % 2:
            step([tiles - 1])

    def forward(places):
        x = jnp.concatenate([x_tile(j).astype(bf16) for j in places], axis=1)
        lattice = jnp.dot(forward_ref[...], x, preferred_element_type=f32).astype(bf16)
        for place, j in enumerate(places):
            lat_ref[j] = lattice[:, place * LANES : (place + 1) * LANES]

    by_pairs(forward)
    copy.wait()
    share = rows // PARTS

    def mix(c, carry):
        part = pl.ds(pl.multiple_of(c * share, share), share)
        half = pl.ds(pl.multiple_of(c % (PARTS // 2) * share, share), share)
        mixed = {}
        for i in range(spans):
            lanes = slice(i * LANES, (i + 1) * LANES)
            source = [
                cut(
                    lambda j: lat_ref[j, part].astype(f32),
                    t * length + i * LANES,
                    min(LANES, length - i * LANES),
                    tiles - 1,
                )
                for t in range(3)
            ]
            for t in range(3):
                summed = (
                    w_ref[2 * t, half, lanes] * source[(t + 1) % 3]
                    + w_ref[2 * t + 1, half, lanes] * source[(t + 2) % 3]
                )
                mixed[t, i] = summed.astype(bf16)
        for j in range(tiles):
            tile = packed(lambda t, i: mixed[t, i].astype(f32), j, 3, length)
            mix_ref[j, part] = tile.astype(bf16)
        return carry

    lax.fori_loop(0, PARTS, mix, 0)

    def backward(places):
        mixed = jnp.concatenate([mix_ref[j] for j in places], axis=1)
        projected = jnp.dot(backward_ref[...], mixed, preferred_element_type=f32).astype(bf16)
        for place, j in enumerate(places):
            turn_ref[place] = x_tile(j)
            for p in range(2):
                half = slice(p * momenta, (p + 1) * momenta)
                part = projected[half, place * LANES : (place + 1) * LANES].astype(f32)
                own = turn_ref[place, pl.ds(p, momenta, stride=2), :]
                out_ref[j, p] = (own + part).astype(bf16)

    by_pairs(backward)


def transform(x, forward, backward, w, length):
    groups, tiles, inner, _ = x.shape
    rows = groups * inner
    return pl.pallas_call(
        functools.partial(transform_kernel, length),
        in_specs=[whole(), whole(), whole(), pl.BlockSpec(memory_space=pl.ANY)],
        out_specs=whole(),
        out_shape=jax.ShapeDtypeStruct((tiles, 2, rows // 2, LANES), jnp.bfloat16),
        scratch_shapes=[
            pltpu.VMEM((tiles, rows, LANES), jnp.bfloat16),
            pltpu.VMEM((tiles, rows, LANES), jnp.bfloat16),
            pltpu.VMEM((2, rows, LANES), jnp.float32),
            pltpu.VMEM(w.shape, jnp.float32),
            pltpu.SemaphoreType.DMA,
        ],
        compiler_params=pltpu.CompilerParams(vmem_limit_bytes=40 * 1024 * 1024),
    )(x, forward, backward, pltpu.with_memory_space_constraint(w, pltpu.HBM))


def products_kernel(t, mine_ref, u_ref, loop_hbm, *refs):
    out_refs, (rows_ref, loop_ref, tall_ref, wide_ref, sem) = refs[:-5], refs[-5:]
    f32, bf16 = jnp.float32, jnp.bfloat16
    mine = mine_ref[0]
    tiles = rows_ref.shape[0]
    cols = len(out_refs)
    groups = u_ref.shape[2] // cols
    order = tall_ref.shape[0] // 2
    narrow = order // groups
    depth = cols * LANES
    row_count = out_refs[0].shape[0]
    first = t * narrow * row_count // LANES
    copy = pltpu.make_async_copy(loop_hbm.at[t], loop_ref, sem)
    copy.start()
    rows_ref[...] = u_ref[first : first + tiles].astype(f32)

    def place(k, carry):
        here = pl.ds(pl.multiple_of(k * LANES, LANES), LANES)
        slab = pl.ds(pl.multiple_of((k ^ mine) * LANES, LANES), LANES)
        there = pl.ds(pl.multiple_of(depth + k * LANES, LANES), LANES)
        for n in range(narrow):
            real, imag = [
                cut(
                    lambda j: rows_ref[j, p, pl.ds(k, groups, stride=cols), :],
                    (t * narrow + n) * row_count - first * LANES,
                    row_count,
                    tiles - 1,
                )
                for p in range(2)
            ]
            minus = (-imag).astype(bf16)
            real, imag = real.astype(bf16), imag.astype(bf16)
            upper = slice(n * groups, (n + 1) * groups)
            lower = slice(order + n * groups, order + (n + 1) * groups)
            tall_ref[upper, slab] = real
            tall_ref[lower, slab] = imag
            wide_ref[upper, here] = real
            wide_ref[upper, there] = minus
            wide_ref[lower, here] = imag
            wide_ref[lower, there] = real
        return carry

    lax.fori_loop(0, cols, place, 0)
    copy.wait()
    middle = lax.dot_general(
        tall_ref[...], loop_ref[...], (((0,), (0,)), ((), ())), preferred_element_type=f32
    ).astype(bf16)
    change = lax.dot_general(
        middle, wide_ref[...], (((1,), (1,)), ((), ())), preferred_element_type=f32
    )
    increment = (step_length * change).astype(bf16)
    for k in range(cols):
        out_refs[k][...] = increment[k * LANES : k * LANES + row_count]


def products(t, mine, u, loops, row_count):
    rows, depth = loops.shape[1:]
    cols = depth // 2 // LANES
    length = rows // 2 // (u.shape[2] // cols) * row_count
    tiles = -(-(t + 1) * length // LANES) - t * length // LANES
    return pl.pallas_call(
        functools.partial(products_kernel, t),
        in_specs=[
            pl.BlockSpec(memory_space=pltpu.SMEM),
            whole(),
            pl.BlockSpec(memory_space=pl.ANY),
        ],
        out_specs=[whole()] * cols,
        out_shape=[jax.ShapeDtypeStruct((row_count, rows), jnp.bfloat16)] * cols,
        scratch_shapes=[
            pltpu.VMEM((tiles,) + u.shape[1:], jnp.float32),
            pltpu.VMEM((rows, depth), jnp.bfloat16),
            pltpu.VMEM((rows, depth // 2), jnp.bfloat16),
            pltpu.VMEM((rows, depth), jnp.bfloat16),
            pltpu.SemaphoreType.DMA,
        ],
        compiler_params=pltpu.CompilerParams(vmem_limit_bytes=32 * 1024 * 1024),
    )(mine, u, pltpu.with_memory_space_constraint(loops, pltpu.HBM))


def finish_kernel(t, count, mine_ref, v_ref, *refs):
    piece_refs, out_hbm, (new_ref, sems) = refs[:count], refs[-3], refs[-2:]
    mine = mine_ref[0]
    copies = []
    for k in range(count):
        q = mine ^ k
        total = v_ref[t, q].astype(jnp.float32) + piece_refs[k][...].astype(jnp.float32)
        new_ref[k] = total.astype(jnp.bfloat16)
        copies.append(pltpu.make_async_copy(new_ref.at[k], out_hbm.at[t, q], sems.at[k]))
        copies[k].start()
    for copy in copies:
        copy.wait()


def finish(t, mine, vertex, pieces, out):
    count = len(pieces)
    operands = [mine, vertex, *pieces]
    specs = [
        pl.BlockSpec(memory_space=pltpu.SMEM),
        whole(),
    ] + [whole()] * count
    aliases = {}
    if out is not None:
        aliases = {len(operands): 0}
        operands.append(out)
        specs.append(pl.BlockSpec(memory_space=pltpu.HBM))
    return pl.pallas_call(
        functools.partial(finish_kernel, t, count),
        in_specs=specs,
        out_specs=pl.BlockSpec(memory_space=pltpu.HBM),
        out_shape=jax.ShapeDtypeStruct(vertex.shape, vertex.dtype),
        input_output_aliases=aliases,
        scratch_shapes=[
            pltpu.VMEM((count,) + vertex.shape[2:], vertex.dtype),
            pltpu.SemaphoreType.DMA((count,)),
        ],
        compiler_params=pltpu.CompilerParams(vmem_limit_bytes=16 * 1024 * 1024),
    )(*operands)


def per_device(vertex, loop_blocks, mixing, bond_offsets):
    groups = lax.axis_size("pb")
    cols = lax.axis_size("col")
    mesh_z = vertex.shape[1]
    row_count = vertex.shape[2]
    order = vertex.shape[3] // 2
    narrow = order // groups
    momenta = mesh_z * groups
    mesh_y = groups // MX
    sent = spread_rows(vertex, groups)
    gathered = lax.all_to_all(sent, "pb", split_axis=0, concat_axis=0, tiled=True)

    forward, backward = phase_tables(momenta, MX, mesh_y, mesh_z)
    forward = forward.transpose(2, 3, 1, 0).reshape(2 * momenta, 2 * momenta)
    backward = backward.transpose(2, 3, 0, 1).reshape(2 * momenta, 2 * momenta)
    bond = jnp.arange(NB, dtype=jnp.int32)
    own = (jnp.arange(narrow, dtype=jnp.int32) * groups + lax.axis_index("pb")) % NB
    column_bonds = jnp.sum(
        jnp.where((own[:, None] == bond[None, :])[:, :, None], bond_offsets[None], 0), axis=1
    )
    w = shifted_weights(mixing, bond_offsets, column_bonds, row_count, (MX, mesh_y, mesh_z))
    lane_pad = LANES - row_count
    loops = loop_blocks.reshape(3, order, 2, cols, row_count)
    loops = jnp.pad(loops, [(0, 0)] * 4 + [(0, lane_pad)]).reshape(3, order, 2, cols * LANES)
    loop_re, loop_im = loops[:, :, 0], loops[:, :, 1]
    loops = jnp.concatenate(
        [
            jnp.concatenate([loop_re, loop_im], axis=2),
            jnp.concatenate([-loop_im, loop_re], axis=2),
        ],
        axis=1,
    )

    united = transform(gathered, forward, backward, w, narrow * row_count)
    united = united.transpose(2, 0, 1, 3)
    sent = lax.all_to_all(united, ("pb", "col"), split_axis=0, concat_axis=0, tiled=True)
    u = sent.transpose(1, 2, 0, 3)
    mine = lax.axis_index("col").astype(jnp.int32).reshape(1)
    parts = []
    for t in range(3):
        if t:
            u, parts[0][1] = lax.optimization_barrier((u, parts[0][1]))
        pieces = list(products(t, mine, u, loops, row_count))
        for k in reversed(range(1, cols)):
            pieces[k] = lax.ppermute(pieces[k], "col", [(i, i ^ k) for i in range(cols)])
        parts.append(pieces)
    out = None
    for t in range(3):
        out = finish(t, mine, vertex, parts[t], out)
    return out


def solution(mesh):
    return jax.shard_map(
        per_device,
        mesh=mesh,
        in_specs=(P(None, "pb", "col", None), P(None, ("pb", "col"), None, None), P(), P()),
        out_specs=P(None, "pb", "col", None),
        check_vma=False,
    )
```

```python
import functools
import math

import jax
import jax.numpy as jnp
from jax import lax
from jax.experimental import pallas as pl
from jax.experimental.pallas import tpu as pltpu
from jax.sharding import PartitionSpec as P

NB = 7
MX = 8
LANES = 128
PARTS = 4


step_length = 0.25


def mesh_coords(momenta, mesh_y, mesh_z):
    flat_index = jnp.arange(momenta, dtype=jnp.int32)
    coord_x = flat_index // (mesh_y * mesh_z)
    coord_y = flat_index // mesh_z % mesh_y
    coord_z = flat_index % mesh_z
    return (coord_x, coord_y, coord_z)


def phase_tables(momenta, mesh_x, mesh_y, mesh_z):
    coord_x, coord_y, coord_z = mesh_coords(momenta, mesh_y, mesh_z)
    phase_index = (
        coord_x[:, None] * coord_x[None, :] * (mesh_y * mesh_z)
        + coord_y[:, None] * coord_y[None, :] * (mesh_x * mesh_z)
        + coord_z[:, None] * coord_z[None, :] * (mesh_x * mesh_y)
    ) % momenta
    angles = phase_index.astype(jnp.float32) * (2.0 * math.pi / momenta)
    cosine = jnp.cos(angles)
    sine_part = jnp.sin(angles)
    forward = jnp.stack([jnp.stack([cosine, sine_part], 1), jnp.stack([-sine_part, cosine], 1)]) * (
        1.0 / momenta
    )
    backward = jnp.stack([jnp.stack([cosine, -sine_part], 1), jnp.stack([sine_part, cosine], 1)])
    return (forward.astype(jnp.bfloat16), backward.astype(jnp.bfloat16))


def pieces_of(values, axis):
    high = lax.reduce_precision(values, 8, 7)
    rest = values - high
    middle = lax.reduce_precision(rest, 8, 7)
    return jnp.concatenate([high, middle, rest - middle], axis=axis).astype(jnp.bfloat16)


def shifted_slots(bond_offsets, sign, sides):
    mesh_x, mesh_y, mesh_z = sides
    coords = mesh_coords(mesh_x * mesh_y * mesh_z, mesh_y, mesh_z)
    slot = 0
    for axis, side in enumerate(sides):
        moved = jnp.mod(coords[axis][None, :] + sign * bond_offsets[:, axis][:, None], side)
        slot = slot * side + moved
    return slot


def shifted_weights(mixing, bond_offsets, column_bonds, row_count, sides):
    count, momenta = mixing.shape
    f32 = jnp.float32
    slots = shifted_slots(bond_offsets, 1, sides)
    source = lax.broadcasted_iota(jnp.int32, (momenta, NB, momenta), 0)
    picks = (source == slots[None]).astype(jnp.bfloat16).reshape(momenta, NB * momenta)
    first = jnp.dot(pieces_of(mixing, 0), picks, preferred_element_type=f32)
    first = first[:count] + first[count : 2 * count] + first[2 * count :]
    first = first.reshape(count * NB, momenta)
    row = lax.broadcasted_iota(jnp.int32, (count * NB, count * LANES), 0)
    lane = lax.broadcasted_iota(jnp.int32, (count * NB, count * LANES), 1)
    spot = lane % LANES
    spread = (row == lane // LANES * NB + spot % NB) & (spot < row_count)
    spread = spread.astype(jnp.bfloat16)
    wide = jnp.dot(pieces_of(first.T, 0), spread, preferred_element_type=f32)
    wide = wide[:momenta] + wide[momenta : 2 * momenta] + wide[2 * momenta :]
    slots = shifted_slots(column_bonds, -1, sides)
    target = lax.broadcasted_iota(jnp.int32, (NB, momenta, momenta), 2)
    picks = (target == slots[:, :, None]).astype(jnp.bfloat16)
    length = NB * row_count
    spans = -(-length // LANES)
    return pl.pallas_call(
        functools.partial(weights_kernel, row_count),
        in_specs=[whole(), whole()],
        out_specs=whole(),
        out_shape=jax.ShapeDtypeStruct((count, momenta, spans * LANES), f32),
        scratch_shapes=[pltpu.VMEM((NB, count, momenta, LANES), f32)],
        compiler_params=pltpu.CompilerParams(vmem_limit_bytes=32 * 1024 * 1024),
    )(picks, pieces_of(wide, 1))


def weights_kernel(row_count, picks_ref, wide_ref, out_ref, tmp_ref):
    count, momenta, _ = out_ref.shape
    width = count * LANES
    spans = out_ref.shape[2] // LANES

    def pick(n, carry):
        both = jnp.dot(picks_ref[n], wide_ref[...], preferred_element_type=jnp.float32)
        both = both[:, :width] + both[:, width : 2 * width] + both[:, 2 * width :]
        for j in range(count):
            tmp_ref[n, j] = both[:, j * LANES : (j + 1) * LANES]
        return carry

    lax.fori_loop(0, NB, pick, 0)
    edge = NB * row_count - (spans - 1) * LANES

    def pack(j, carry):
        for i in range(spans):
            tile = packed(lambda s, _: tmp_ref[s, j], i, NB, row_count)
            if i == spans - 1:
                tile = jnp.where(lane_ids(momenta) < edge, tile, 0.0)
            out_ref[j, :, i * LANES : (i + 1) * LANES] = tile
        return carry

    lax.fori_loop(0, count, pack, 0)


def lane_ids(rows):
    return lax.broadcasted_iota(jnp.int32, (rows, LANES), 1)


def moved(tile, shift):
    shift = shift % LANES
    return pltpu.roll(tile, shift, 1) if shift else tile


def cut(get, start, length, last):
    index, offset = divmod(start, LANES)
    tile = moved(get(index), -offset)
    if offset + length <= LANES or index == last:
        return tile
    rest = moved(get(index + 1), LANES - offset)
    return jnp.where(lane_ids(tile.shape[0]) < LANES - offset, tile, rest)


def packed(get, j, segments, length):
    low, high = j * LANES, (j + 1) * LANES
    out = None
    for s in range(segments):
        for i in range(-(-length // LANES)):
            first = s * length + i * LANES
            stop = s * length + min((i + 1) * LANES, length)
            if stop <= low or first >= high:
                continue
            tile = moved(get(s, i), first - low)
            begin = max(first, low) - low
            out = tile if out is None else jnp.where(lane_ids(tile.shape[0]) < begin, out, tile)
    return out


def spread_kernel(v_hbm, out_hbm, v_ref, tmp_ref, out_ref, in_sems, out_sems):
    channels, mesh_z, row_count, width = v_ref.shape
    groups, tiles, inner, _ = out_ref.shape
    order = width // 2
    narrow = order // groups
    share = groups // PARTS
    arriving = [
        pltpu.make_async_copy(v_hbm.at[t], v_ref.at[t], in_sems.at[t]) for t in range(channels)
    ]
    for copy in arriving:
        copy.start()

    for t in range(channels):
        arriving[t].wait()

        for z in range(mesh_z):
            block = v_ref[t, z].astype(jnp.float32)
            zeros = jnp.zeros((LANES - row_count, width), jnp.float32)
            turned = jnp.concatenate([block, zeros], axis=0).T
            for p in range(2):
                for n in range(narrow):
                    start = p * order + n * groups
                    tmp_ref[t * narrow + n, pl.ds(2 * z + p, groups, stride=inner), :] = turned[
                        start : start + groups
                    ]

    leaving = []
    for c in range(PARTS):
        part = pl.ds(c * share, share)
        leaving.append(pltpu.make_async_copy(out_ref.at[part], out_hbm.at[part], out_sems.at[c]))
        rows = pl.ds(c * share * inner, share * inner)
        for j in range(tiles):
            tile = packed(lambda s, i: tmp_ref[s, rows], j, channels * narrow, row_count)
            out_ref[part, j] = tile.reshape(share, inner, LANES).astype(jnp.bfloat16)
        leaving[c].start()
    for copy in leaving:
        copy.wait()


def whole():
    return pl.BlockSpec(memory_space=pltpu.VMEM)


def spread_rows(vertex, groups):
    channels, mesh_z, row_count, width = vertex.shape
    narrow = width // 2 // groups
    tiles = -(-channels * narrow * row_count // LANES)
    shape = (groups, tiles, 2 * mesh_z, LANES)
    return pl.pallas_call(
        spread_kernel,
        in_specs=[pl.BlockSpec(memory_space=pltpu.HBM)],
        out_specs=pl.BlockSpec(memory_space=pltpu.HBM),
        out_shape=pltpu.HBM(shape, jnp.bfloat16),
        scratch_shapes=[
            pltpu.VMEM(vertex.shape, jnp.bfloat16),
            pltpu.VMEM((channels * narrow, groups * 2 * mesh_z, LANES), jnp.float32),
            pltpu.VMEM(shape, jnp.bfloat16),
            pltpu.SemaphoreType.DMA((channels,)),
            pltpu.SemaphoreType.DMA((PARTS,)),
        ],
        compiler_params=pltpu.CompilerParams(vmem_limit_bytes=32 * 1024 * 1024),
    )(pltpu.with_memory_space_constraint(vertex, pltpu.HBM))


def transform_kernel(
    length, x_ref, forward_ref, backward_ref, w_hbm, out_ref, lat_ref, mix_ref, w_ref, sem
):
    f32, bf16 = jnp.float32, jnp.bfloat16
    rows = forward_ref.shape[0]
    tiles = x_ref.shape[1]
    spans = -(-length // LANES)
    copy = pltpu.make_async_copy(w_hbm, w_ref, sem)
    copy.start()

    def x_tile(j):
        return x_ref[:, j].astype(f32).reshape(rows, LANES)

    def by_pairs(step):
        def pair(i, carry):
            step([2 * i, 2 * i + 1])
            return carry

        lax.fori_loop(0, tiles // 2, pair, 0, unroll=3)
        if tiles % 2:
            step([tiles - 1])

    def forward(places):
        x = jnp.concatenate([x_tile(j).astype(bf16) for j in places], axis=1)
        lattice = jnp.dot(forward_ref[...], x, preferred_element_type=f32).astype(bf16)
        for place, j in enumerate(places):
            lat_ref[j] = lattice[:, place * LANES : (place + 1) * LANES]

    by_pairs(forward)
    copy.wait()
    share = rows // PARTS

    def mix(c, carry):
        part = pl.ds(pl.multiple_of(c * share, share), share)
        half = pl.ds(pl.multiple_of(c % (PARTS // 2) * share, share), share)
        mixed = {}
        for i in range(spans):
            lanes = slice(i * LANES, (i + 1) * LANES)
            source = [
                cut(
                    lambda j: lat_ref[j, part].astype(f32),
                    t * length + i * LANES,
                    min(LANES, length - i * LANES),
                    tiles - 1,
                )
                for t in range(3)
            ]
            for t in range(3):
                summed = (
                    w_ref[2 * t, half, lanes] * source[(t + 1) % 3]
                    + w_ref[2 * t + 1, half, lanes] * source[(t + 2) % 3]
                )
                mixed[t, i] = summed.astype(bf16)
        for j in range(tiles):
            tile = packed(lambda t, i: mixed[t, i].astype(f32), j, 3, length)
            mix_ref[j, part] = tile.astype(bf16)
        return carry

    lax.fori_loop(0, PARTS, mix, 0)

    def backward(places):
        mixed = jnp.concatenate([mix_ref[j] for j in places], axis=1)
        projected = jnp.dot(backward_ref[...], mixed, preferred_element_type=f32).astype(bf16)
        for place, j in enumerate(places):
            part = projected[:, place * LANES : (place + 1) * LANES].astype(f32)
            out_ref[j] = (x_tile(j) + part).astype(bf16)

    by_pairs(backward)


def transform(x, forward, backward, w, length):
    groups, tiles, inner, _ = x.shape
    rows = groups * inner
    return pl.pallas_call(
        functools.partial(transform_kernel, length),
        in_specs=[whole(), whole(), whole(), pl.BlockSpec(memory_space=pl.ANY)],
        out_specs=whole(),
        out_shape=jax.ShapeDtypeStruct((tiles, rows, LANES), jnp.bfloat16),
        scratch_shapes=[
            pltpu.VMEM((tiles, rows, LANES), jnp.bfloat16),
            pltpu.VMEM((tiles, rows, LANES), jnp.bfloat16),
            pltpu.VMEM(w.shape, jnp.float32),
            pltpu.SemaphoreType.DMA,
        ],
        compiler_params=pltpu.CompilerParams(vmem_limit_bytes=28 * 1024 * 1024),
    )(x, forward, backward, pltpu.with_memory_space_constraint(w, pltpu.HBM))


def products_kernel(t, mine_ref, u_ref, loop_hbm, *refs):
    out_refs, (rows_ref, loop_ref, tall_ref, wide_ref, sem) = refs[:-5], refs[-5:]
    f32, bf16 = jnp.float32, jnp.bfloat16
    mine = mine_ref[0]
    tiles = rows_ref.shape[0]
    cols = len(out_refs)
    groups = u_ref.shape[2] // cols
    order = tall_ref.shape[0] // 2
    narrow = order // groups
    depth = cols * LANES
    row_count = out_refs[0].shape[0]
    first = t * narrow * row_count // LANES
    copy = pltpu.make_async_copy(loop_hbm.at[t], loop_ref, sem)
    copy.start()
    rows_ref[...] = u_ref[first : first + tiles].astype(f32)

    def place(k, carry):
        here = pl.ds(pl.multiple_of(k * LANES, LANES), LANES)
        slab = pl.ds(pl.multiple_of((k ^ mine) * LANES, LANES), LANES)
        there = pl.ds(pl.multiple_of(depth + k * LANES, LANES), LANES)
        for n in range(narrow):
            real, imag = [
                cut(
                    lambda j: rows_ref[j, p, pl.ds(k, groups, stride=cols), :],
                    (t * narrow + n) * row_count - first * LANES,
                    row_count,
                    tiles - 1,
                )
                for p in range(2)
            ]
            minus = (-imag).astype(bf16)
            real, imag = real.astype(bf16), imag.astype(bf16)
            upper = slice(n * groups, (n + 1) * groups)
            lower = slice(order + n * groups, order + (n + 1) * groups)
            tall_ref[upper, slab] = real
            tall_ref[lower, slab] = imag
            wide_ref[upper, here] = real
            wide_ref[upper, there] = minus
            wide_ref[lower, here] = imag
            wide_ref[lower, there] = real
        return carry

    lax.fori_loop(0, cols, place, 0)
    copy.wait()
    middle = lax.dot_general(
        tall_ref[...], loop_ref[...], (((0,), (0,)), ((), ())), preferred_element_type=f32
    ).astype(bf16)
    change = lax.dot_general(
        middle, wide_ref[...], (((1,), (1,)), ((), ())), preferred_element_type=f32
    )
    increment = (step_length * change).astype(bf16)
    for k in range(cols):
        out_refs[k][...] = increment[k * LANES : k * LANES + row_count]


def products(t, mine, u, loops, row_count):
    rows, depth = loops.shape[1:]
    cols = depth // 2 // LANES
    length = rows // 2 // (u.shape[2] // cols) * row_count
    tiles = -(-(t + 1) * length // LANES) - t * length // LANES
    return pl.pallas_call(
        functools.partial(products_kernel, t),
        in_specs=[
            pl.BlockSpec(memory_space=pltpu.SMEM),
            whole(),
            pl.BlockSpec(memory_space=pl.ANY),
        ],
        out_specs=[whole()] * cols,
        out_shape=[jax.ShapeDtypeStruct((row_count, rows), jnp.bfloat16)] * cols,
        scratch_shapes=[
            pltpu.VMEM((tiles,) + u.shape[1:], jnp.float32),
            pltpu.VMEM((rows, depth), jnp.bfloat16),
            pltpu.VMEM((rows, depth // 2), jnp.bfloat16),
            pltpu.VMEM((rows, depth), jnp.bfloat16),
            pltpu.SemaphoreType.DMA,
        ],
        compiler_params=pltpu.CompilerParams(vmem_limit_bytes=32 * 1024 * 1024),
    )(mine, u, pltpu.with_memory_space_constraint(loops, pltpu.HBM))


def finish_kernel(t, count, mine_ref, v_ref, *refs):
    piece_refs, out_hbm, (new_ref, sems) = refs[:count], refs[-3], refs[-2:]
    mine = mine_ref[0]
    copies = []
    for k in range(count):
        q = mine ^ k
        total = v_ref[t, q].astype(jnp.float32) + piece_refs[k][...].astype(jnp.float32)
        new_ref[k] = total.astype(jnp.bfloat16)
        copies.append(pltpu.make_async_copy(new_ref.at[k], out_hbm.at[t, q], sems.at[k]))
        copies[k].start()
    for copy in copies:
        copy.wait()


def finish(t, mine, vertex, pieces, out):
    count = len(pieces)
    operands = [mine, vertex, *pieces]
    specs = [
        pl.BlockSpec(memory_space=pltpu.SMEM),
        whole(),
    ] + [whole()] * count
    aliases = {}
    if out is not None:
        aliases = {len(operands): 0}
        operands.append(out)
        specs.append(pl.BlockSpec(memory_space=pltpu.HBM))
    return pl.pallas_call(
        functools.partial(finish_kernel, t, count),
        in_specs=specs,
        out_specs=pl.BlockSpec(memory_space=pltpu.HBM),
        out_shape=jax.ShapeDtypeStruct(vertex.shape, vertex.dtype),
        input_output_aliases=aliases,
        scratch_shapes=[
            pltpu.VMEM((count,) + vertex.shape[2:], vertex.dtype),
            pltpu.SemaphoreType.DMA((count,)),
        ],
        compiler_params=pltpu.CompilerParams(vmem_limit_bytes=16 * 1024 * 1024),
    )(*operands)


def per_device(vertex, loop_blocks, mixing, bond_offsets):
    groups = lax.axis_size("pb")
    cols = lax.axis_size("col")
    mesh_z = vertex.shape[1]
    row_count = vertex.shape[2]
    order = vertex.shape[3] // 2
    narrow = order // groups
    momenta = mesh_z * groups
    mesh_y = groups // MX
    sent = spread_rows(vertex, groups)
    gathered = lax.all_to_all(sent, "pb", split_axis=0, concat_axis=0, tiled=True)

    forward, backward = phase_tables(momenta, MX, mesh_y, mesh_z)
    forward = forward.transpose(2, 3, 1, 0).reshape(2 * momenta, 2 * momenta)
    backward = backward.transpose(3, 2, 0, 1).reshape(2 * momenta, 2 * momenta)
    bond = jnp.arange(NB, dtype=jnp.int32)
    own = (jnp.arange(narrow, dtype=jnp.int32) * groups + lax.axis_index("pb")) % NB
    column_bonds = jnp.sum(
        jnp.where((own[:, None] == bond[None, :])[:, :, None], bond_offsets[None], 0), axis=1
    )
    w = shifted_weights(mixing, bond_offsets, column_bonds, row_count, (MX, mesh_y, mesh_z))
    lane_pad = LANES - row_count
    loops = loop_blocks.reshape(3, order, 2, cols, row_count)
    loops = jnp.pad(loops, [(0, 0)] * 4 + [(0, lane_pad)]).reshape(3, order, 2, cols * LANES)
    loop_re, loop_im = loops[:, :, 0], loops[:, :, 1]
    loops = jnp.concatenate(
        [
            jnp.concatenate([loop_re, loop_im], axis=2),
            jnp.concatenate([-loop_im, loop_re], axis=2),
        ],
        axis=1,
    )

    gathered, loops = lax.optimization_barrier((gathered, loops))
    united = transform(gathered, forward, backward, w, narrow * row_count)
    tiles = united.shape[0]
    united = united.reshape(tiles, momenta, 2, LANES).transpose(1, 0, 2, 3)
    sent = lax.all_to_all(united, ("pb", "col"), split_axis=0, concat_axis=0, tiled=True)
    u = sent.transpose(1, 2, 0, 3)
    mine = lax.axis_index("col").astype(jnp.int32).reshape(1)
    parts = []
    for t in range(3):
        if t:
            u, parts[0][1] = lax.optimization_barrier((u, parts[0][1]))
        pieces = list(products(t, mine, u, loops, row_count))
        for k in reversed(range(1, cols)):
            pieces[k] = lax.ppermute(pieces[k], "col", [(i, i ^ k) for i in range(cols)])
        parts.append(pieces)
    out = None
    for t in range(3):
        out = finish(t, mine, vertex, parts[t], out)
    return out


def solution(mesh):
    return jax.shard_map(
        per_device,
        mesh=mesh,
        in_specs=(P(None, "pb", "col", None), P(None, ("pb", "col"), None, None), P(), P()),
        out_specs=P(None, "pb", "col", None),
        check_vma=False,
    )
```

```python
import functools
import math

import jax
import jax.numpy as jnp
from jax import lax
from jax.experimental import pallas as pl
from jax.experimental.pallas import tpu as pltpu
from jax.sharding import PartitionSpec as P

NB = 7
MX = 8
LANES = 128
PARTS = 4


step_length = 0.25


def mesh_coords(momenta, mesh_y, mesh_z):
    flat_index = jnp.arange(momenta, dtype=jnp.int32)
    coord_x = flat_index // (mesh_y * mesh_z)
    coord_y = flat_index // mesh_z % mesh_y
    coord_z = flat_index % mesh_z
    return (coord_x, coord_y, coord_z)


def phase_tables(momenta, mesh_x, mesh_y, mesh_z):
    coord_x, coord_y, coord_z = mesh_coords(momenta, mesh_y, mesh_z)
    phase_index = (
        coord_x[:, None] * coord_x[None, :] * (mesh_y * mesh_z)
        + coord_y[:, None] * coord_y[None, :] * (mesh_x * mesh_z)
        + coord_z[:, None] * coord_z[None, :] * (mesh_x * mesh_y)
    ) % momenta
    angles = phase_index.astype(jnp.float32) * (2.0 * math.pi / momenta)
    cosine = jnp.cos(angles)
    sine_part = jnp.sin(angles)
    forward = jnp.stack([jnp.stack([cosine, sine_part], 1), jnp.stack([-sine_part, cosine], 1)]) * (
        1.0 / momenta
    )
    backward = jnp.stack([jnp.stack([cosine, -sine_part], 1), jnp.stack([sine_part, cosine], 1)])
    return (forward.astype(jnp.bfloat16), backward.astype(jnp.bfloat16))


def pieces_of(values, axis):
    high = lax.reduce_precision(values, 8, 7)
    rest = values - high
    middle = lax.reduce_precision(rest, 8, 7)
    return jnp.concatenate([high, middle, rest - middle], axis=axis).astype(jnp.bfloat16)


def shifted_slots(bond_offsets, sign, sides):
    mesh_x, mesh_y, mesh_z = sides
    coords = mesh_coords(mesh_x * mesh_y * mesh_z, mesh_y, mesh_z)
    slot = 0
    for axis, side in enumerate(sides):
        moved = jnp.mod(coords[axis][None, :] + sign * bond_offsets[:, axis][:, None], side)
        slot = slot * side + moved
    return slot


def shifted_weights(mixing, bond_offsets, column_bonds, row_count, sides):
    count, momenta = mixing.shape
    f32 = jnp.float32
    slots = shifted_slots(bond_offsets, 1, sides)
    source = lax.broadcasted_iota(jnp.int32, (momenta, NB, momenta), 0)
    picks = (source == slots[None]).astype(jnp.bfloat16).reshape(momenta, NB * momenta)
    first = jnp.dot(pieces_of(mixing, 0), picks, preferred_element_type=f32)
    first = first[:count] + first[count : 2 * count] + first[2 * count :]
    first = first.reshape(count * NB, momenta)
    row = lax.broadcasted_iota(jnp.int32, (count * NB, count * LANES), 0)
    lane = lax.broadcasted_iota(jnp.int32, (count * NB, count * LANES), 1)
    spot = lane % LANES
    spread = (row == lane // LANES * NB + spot % NB) & (spot < row_count)
    spread = spread.astype(jnp.bfloat16)
    wide = jnp.dot(pieces_of(first.T, 0), spread, preferred_element_type=f32)
    wide = wide[:momenta] + wide[momenta : 2 * momenta] + wide[2 * momenta :]
    slots = shifted_slots(column_bonds, -1, sides)
    target = lax.broadcasted_iota(jnp.int32, (NB, momenta, momenta), 2)
    picks = (target == slots[:, :, None]).astype(jnp.bfloat16)
    length = NB * row_count
    spans = -(-length // LANES)
    return pl.pallas_call(
        functools.partial(weights_kernel, row_count),
        in_specs=[whole(), whole()],
        out_specs=whole(),
        out_shape=jax.ShapeDtypeStruct((count, momenta, spans * LANES), f32),
        scratch_shapes=[pltpu.VMEM((NB, count, momenta, LANES), f32)],
        compiler_params=pltpu.CompilerParams(vmem_limit_bytes=32 * 1024 * 1024),
    )(picks, pieces_of(wide, 1))


def weights_kernel(row_count, picks_ref, wide_ref, out_ref, tmp_ref):
    count, momenta, _ = out_ref.shape
    width = count * LANES
    spans = out_ref.shape[2] // LANES

    def pick(n, carry):
        both = jnp.dot(picks_ref[n], wide_ref[...], preferred_element_type=jnp.float32)
        both = both[:, :width] + both[:, width : 2 * width] + both[:, 2 * width :]
        for j in range(count):
            tmp_ref[n, j] = both[:, j * LANES : (j + 1) * LANES]
        return carry

    lax.fori_loop(0, NB, pick, 0)
    edge = NB * row_count - (spans - 1) * LANES

    def pack(j, carry):
        for i in range(spans):
            tile = packed(lambda s, _: tmp_ref[s, j], i, NB, row_count)
            if i == spans - 1:
                tile = jnp.where(lane_ids(momenta) < edge, tile, 0.0)
            out_ref[j, :, i * LANES : (i + 1) * LANES] = tile
        return carry

    lax.fori_loop(0, count, pack, 0)


def lane_ids(rows):
    return lax.broadcasted_iota(jnp.int32, (rows, LANES), 1)


def moved(tile, shift):
    shift = shift % LANES
    return pltpu.roll(tile, shift, 1) if shift else tile


def cut(get, start, length, last):
    index, offset = divmod(start, LANES)
    tile = moved(get(index), -offset)
    if offset + length <= LANES or index == last:
        return tile
    rest = moved(get(index + 1), LANES - offset)
    return jnp.where(lane_ids(tile.shape[0]) < LANES - offset, tile, rest)


def packed(get, j, segments, length):
    low, high = j * LANES, (j + 1) * LANES
    out = None
    for s in range(segments):
        for i in range(-(-length // LANES)):
            first = s * length + i * LANES
            stop = s * length + min((i + 1) * LANES, length)
            if stop <= low or first >= high:
                continue
            tile = moved(get(s, i), first - low)
            begin = max(first, low) - low
            out = tile if out is None else jnp.where(lane_ids(tile.shape[0]) < begin, out, tile)
    return out


def spread_kernel(v_hbm, out_hbm, v_ref, tmp_ref, out_ref, in_sems, out_sems):
    channels, mesh_z, row_count, width = v_ref.shape
    groups, tiles, inner, _ = out_ref.shape
    order = width // 2
    narrow = order // groups
    share = groups // PARTS
    arriving = [
        pltpu.make_async_copy(v_hbm.at[t], v_ref.at[t], in_sems.at[t]) for t in range(channels)
    ]
    for copy in arriving:
        copy.start()

    for t in range(channels):
        arriving[t].wait()

        for z in range(mesh_z):
            block = v_ref[t, z].astype(jnp.float32)
            zeros = jnp.zeros((LANES - row_count, width), jnp.float32)
            turned = jnp.concatenate([block, zeros], axis=0).T
            for p in range(2):
                for n in range(narrow):
                    start = p * order + n * groups
                    tmp_ref[t * narrow + n, pl.ds(2 * z + p, groups, stride=inner), :] = turned[
                        start : start + groups
                    ]

    leaving = []
    for c in range(PARTS):
        part = pl.ds(c * share, share)
        leaving.append(pltpu.make_async_copy(out_ref.at[part], out_hbm.at[part], out_sems.at[c]))
        rows = pl.ds(c * share * inner, share * inner)
        for j in range(tiles):
            tile = packed(lambda s, i: tmp_ref[s, rows], j, channels * narrow, row_count)
            out_ref[part, j] = tile.reshape(share, inner, LANES).astype(jnp.bfloat16)
        leaving[c].start()
    for copy in leaving:
        copy.wait()


def whole():
    return pl.BlockSpec(memory_space=pltpu.VMEM)


def spread_rows(vertex, groups):
    channels, mesh_z, row_count, width = vertex.shape
    narrow = width // 2 // groups
    tiles = -(-channels * narrow * row_count // LANES)
    shape = (groups, tiles, 2 * mesh_z, LANES)
    return pl.pallas_call(
        spread_kernel,
        in_specs=[pl.BlockSpec(memory_space=pltpu.HBM)],
        out_specs=pl.BlockSpec(memory_space=pltpu.HBM),
        out_shape=pltpu.HBM(shape, jnp.bfloat16),
        scratch_shapes=[
            pltpu.VMEM(vertex.shape, jnp.bfloat16),
            pltpu.VMEM((channels * narrow, groups * 2 * mesh_z, LANES), jnp.float32),
            pltpu.VMEM(shape, jnp.bfloat16),
            pltpu.SemaphoreType.DMA((channels,)),
            pltpu.SemaphoreType.DMA((PARTS,)),
        ],
        compiler_params=pltpu.CompilerParams(vmem_limit_bytes=32 * 1024 * 1024),
    )(pltpu.with_memory_space_constraint(vertex, pltpu.HBM))


def transform_kernel(
    length, x_ref, forward_ref, backward_ref, w_hbm, out_hbm, lat_ref, mix_ref, out_ref, w_ref, sem, out_sems
):
    f32, bf16 = jnp.float32, jnp.bfloat16
    rows = forward_ref.shape[0]
    tiles = x_ref.shape[1]
    spans = -(-length // LANES)
    copy = pltpu.make_async_copy(w_hbm, w_ref, sem)
    copy.start()

    def x_tile(j):
        return x_ref[:, j].astype(f32).reshape(rows, LANES)

    def by_pairs(step):
        def pair(i, carry):
            step([2 * i, 2 * i + 1])
            return carry

        lax.fori_loop(0, tiles // 2, pair, 0, unroll=3)
        if tiles % 2:
            step([tiles - 1])

    def forward(places):
        x = jnp.concatenate([x_tile(j).astype(bf16) for j in places], axis=1)
        lattice = jnp.dot(forward_ref[...], x, preferred_element_type=f32).astype(bf16)
        for place, j in enumerate(places):
            lat_ref[j] = lattice[:, place * LANES : (place + 1) * LANES]

    by_pairs(forward)
    copy.wait()
    share = rows // PARTS

    def mix(c, carry):
        part = pl.ds(pl.multiple_of(c * share, share), share)
        half = pl.ds(pl.multiple_of(c % (PARTS // 2) * share, share), share)
        mixed = {}
        for i in range(spans):
            lanes = slice(i * LANES, (i + 1) * LANES)
            source = [
                cut(
                    lambda j: lat_ref[j, part].astype(f32),
                    t * length + i * LANES,
                    min(LANES, length - i * LANES),
                    tiles - 1,
                )
                for t in range(3)
            ]
            for t in range(3):
                summed = (
                    w_ref[2 * t, half, lanes] * source[(t + 1) % 3]
                    + w_ref[2 * t + 1, half, lanes] * source[(t + 2) % 3]
                )
                mixed[t, i] = summed.astype(bf16)
        for j in range(tiles):
            tile = packed(lambda t, i: mixed[t, i].astype(f32), j, 3, length)
            mix_ref[j, part] = tile.astype(bf16)
        return carry

    lax.fori_loop(0, PARTS, mix, 0)

    def backward(places):
        mixed = jnp.concatenate([mix_ref[j] for j in places], axis=1)
        projected = jnp.dot(backward_ref[...], mixed, preferred_element_type=f32).astype(bf16)
        for place, j in enumerate(places):
            part = projected[:, place * LANES : (place + 1) * LANES].astype(f32)
            united = (x_tile(j) + part).astype(bf16)
            out_ref[j] = united.reshape(rows // 2, 2, LANES)
            leaving(j).start()

    def leaving(j):
        return pltpu.make_async_copy(out_ref.at[j], out_hbm.at[:, j], out_sems.at[j])

    by_pairs(backward)
    for j in range(tiles):
        leaving(j).wait()


def transform(x, forward, backward, w, length):
    groups, tiles, inner, _ = x.shape
    rows = groups * inner
    return pl.pallas_call(
        functools.partial(transform_kernel, length),
        in_specs=[whole(), whole(), whole(), pl.BlockSpec(memory_space=pl.ANY)],
        out_specs=pl.BlockSpec(memory_space=pltpu.HBM),
        out_shape=pltpu.HBM((rows // 2, tiles, 2, LANES), jnp.bfloat16),
        scratch_shapes=[
            pltpu.VMEM((tiles, rows, LANES), jnp.bfloat16),
            pltpu.VMEM((tiles, rows, LANES), jnp.bfloat16),
            pltpu.VMEM((tiles, rows // 2, 2, LANES), jnp.bfloat16),
            pltpu.VMEM(w.shape, jnp.float32),
            pltpu.SemaphoreType.DMA,
            pltpu.SemaphoreType.DMA((tiles,)),
        ],
        compiler_params=pltpu.CompilerParams(vmem_limit_bytes=28 * 1024 * 1024),
    )(x, forward, backward, pltpu.with_memory_space_constraint(w, pltpu.HBM))


def products_kernel(t, mine_ref, u_ref, loop_hbm, *refs):
    out_refs, (rows_ref, loop_ref, tall_ref, wide_ref, sem) = refs[:-5], refs[-5:]
    f32, bf16 = jnp.float32, jnp.bfloat16
    mine = mine_ref[0]
    tiles = rows_ref.shape[0]
    cols = len(out_refs)
    groups = u_ref.shape[2] // cols
    order = tall_ref.shape[0] // 2
    narrow = order // groups
    depth = cols * LANES
    row_count = out_refs[0].shape[0]
    first = t * narrow * row_count // LANES
    copy = pltpu.make_async_copy(loop_hbm.at[t], loop_ref, sem)
    copy.start()
    rows_ref[...] = u_ref[first : first + tiles].astype(f32)

    def place(k, carry):
        here = pl.ds(pl.multiple_of(k * LANES, LANES), LANES)
        slab = pl.ds(pl.multiple_of((k ^ mine) * LANES, LANES), LANES)
        there = pl.ds(pl.multiple_of(depth + k * LANES, LANES), LANES)
        for n in range(narrow):
            real, imag = [
                cut(
                    lambda j: rows_ref[j, p, pl.ds(k, groups, stride=cols), :],
                    (t * narrow + n) * row_count - first * LANES,
                    row_count,
                    tiles - 1,
                )
                for p in range(2)
            ]
            minus = (-imag).astype(bf16)
            real, imag = real.astype(bf16), imag.astype(bf16)
            upper = slice(n * groups, (n + 1) * groups)
            lower = slice(order + n * groups, order + (n + 1) * groups)
            tall_ref[upper, slab] = real
            tall_ref[lower, slab] = imag
            wide_ref[upper, here] = real
            wide_ref[upper, there] = minus
            wide_ref[lower, here] = imag
            wide_ref[lower, there] = real
        return carry

    lax.fori_loop(0, cols, place, 0)
    copy.wait()
    middle = lax.dot_general(
        tall_ref[...], loop_ref[...], (((0,), (0,)), ((), ())), preferred_element_type=f32
    ).astype(bf16)
    change = lax.dot_general(
        middle, wide_ref[...], (((1,), (1,)), ((), ())), preferred_element_type=f32
    )
    increment = (step_length * change).astype(bf16)
    for k in range(cols):
        out_refs[k][...] = increment[k * LANES : k * LANES + row_count]


def products(t, mine, u, loops, row_count):
    rows, depth = loops.shape[1:]
    cols = depth // 2 // LANES
    length = rows // 2 // (u.shape[2] // cols) * row_count
    tiles = -(-(t + 1) * length // LANES) - t * length // LANES
    return pl.pallas_call(
        functools.partial(products_kernel, t),
        in_specs=[
            pl.BlockSpec(memory_space=pltpu.SMEM),
            whole(),
            pl.BlockSpec(memory_space=pl.ANY),
        ],
        out_specs=[whole()] * cols,
        out_shape=[jax.ShapeDtypeStruct((row_count, rows), jnp.bfloat16)] * cols,
        scratch_shapes=[
            pltpu.VMEM((tiles,) + u.shape[1:], jnp.float32),
            pltpu.VMEM((rows, depth), jnp.bfloat16),
            pltpu.VMEM((rows, depth // 2), jnp.bfloat16),
            pltpu.VMEM((rows, depth), jnp.bfloat16),
            pltpu.SemaphoreType.DMA,
        ],
        compiler_params=pltpu.CompilerParams(vmem_limit_bytes=32 * 1024 * 1024),
    )(mine, u, pltpu.with_memory_space_constraint(loops, pltpu.HBM))


def finish_kernel(t, count, mine_ref, v_ref, *refs):
    piece_refs, out_hbm, (new_ref, sems) = refs[:count], refs[-3], refs[-2:]
    mine = mine_ref[0]
    copies = []
    for k in range(count):
        q = mine ^ k
        total = v_ref[t, q].astype(jnp.float32) + piece_refs[k][...].astype(jnp.float32)
        new_ref[k] = total.astype(jnp.bfloat16)
        copies.append(pltpu.make_async_copy(new_ref.at[k], out_hbm.at[t, q], sems.at[k]))
        copies[k].start()
    for copy in copies:
        copy.wait()


def finish(t, mine, vertex, pieces, out):
    count = len(pieces)
    operands = [mine, vertex, *pieces]
    specs = [
        pl.BlockSpec(memory_space=pltpu.SMEM),
        whole(),
    ] + [whole()] * count
    aliases = {}
    if out is not None:
        aliases = {len(operands): 0}
        operands.append(out)
        specs.append(pl.BlockSpec(memory_space=pltpu.HBM))
    return pl.pallas_call(
        functools.partial(finish_kernel, t, count),
        in_specs=specs,
        out_specs=pl.BlockSpec(memory_space=pltpu.HBM),
        out_shape=jax.ShapeDtypeStruct(vertex.shape, vertex.dtype),
        input_output_aliases=aliases,
        scratch_shapes=[
            pltpu.VMEM((count,) + vertex.shape[2:], vertex.dtype),
            pltpu.SemaphoreType.DMA((count,)),
        ],
        compiler_params=pltpu.CompilerParams(vmem_limit_bytes=16 * 1024 * 1024),
    )(*operands)


def per_device(vertex, loop_blocks, mixing, bond_offsets):
    groups = lax.axis_size("pb")
    cols = lax.axis_size("col")
    mesh_z = vertex.shape[1]
    row_count = vertex.shape[2]
    order = vertex.shape[3] // 2
    narrow = order // groups
    momenta = mesh_z * groups
    mesh_y = groups // MX
    sent = spread_rows(vertex, groups)
    gathered = lax.all_to_all(sent, "pb", split_axis=0, concat_axis=0, tiled=True)

    forward, backward = phase_tables(momenta, MX, mesh_y, mesh_z)
    forward = forward.transpose(2, 3, 1, 0).reshape(2 * momenta, 2 * momenta)
    backward = backward.transpose(3, 2, 0, 1).reshape(2 * momenta, 2 * momenta)
    bond = jnp.arange(NB, dtype=jnp.int32)
    own = (jnp.arange(narrow, dtype=jnp.int32) * groups + lax.axis_index("pb")) % NB
    column_bonds = jnp.sum(
        jnp.where((own[:, None] == bond[None, :])[:, :, None], bond_offsets[None], 0), axis=1
    )
    w = shifted_weights(mixing, bond_offsets, column_bonds, row_count, (MX, mesh_y, mesh_z))
    lane_pad = LANES - row_count
    loops = loop_blocks.reshape(3, order, 2, cols, row_count)
    loops = jnp.pad(loops, [(0, 0)] * 4 + [(0, lane_pad)]).reshape(3, order, 2, cols * LANES)
    loop_re, loop_im = loops[:, :, 0], loops[:, :, 1]
    loops = jnp.concatenate(
        [
            jnp.concatenate([loop_re, loop_im], axis=2),
            jnp.concatenate([-loop_im, loop_re], axis=2),
        ],
        axis=1,
    )

    gathered, loops = lax.optimization_barrier((gathered, loops))
    united = transform(gathered, forward, backward, w, narrow * row_count)
    sent = lax.all_to_all(united, ("pb", "col"), split_axis=0, concat_axis=0, tiled=True)
    u = sent.transpose(1, 2, 0, 3)
    mine = lax.axis_index("col").astype(jnp.int32).reshape(1)
    parts = []
    for t in range(3):
        if t:
            u, parts[0][1] = lax.optimization_barrier((u, parts[0][1]))
        pieces = list(products(t, mine, u, loops, row_count))
        for k in reversed(range(1, cols)):
            pieces[k] = lax.ppermute(pieces[k], "col", [(i, i ^ k) for i in range(cols)])
        parts.append(pieces)
    out = None
    for t in range(3):
        out = finish(t, mine, vertex, parts[t], out)
    return out


def solution(mesh):
    return jax.shard_map(
        per_device,
        mesh=mesh,
        in_specs=(P(None, "pb", "col", None), P(None, ("pb", "col"), None, None), P(), P()),
        out_specs=P(None, "pb", "col", None),
        check_vma=False,
    )
```

```python
import functools
import math

import jax
import jax.numpy as jnp
from jax import lax
from jax.experimental import pallas as pl
from jax.experimental.pallas import tpu as pltpu
from jax.sharding import PartitionSpec as P

NB = 7
MX = 8
LANES = 128
PARTS = 4


step_length = 0.25


def mesh_coords(momenta, mesh_y, mesh_z):
    flat_index = jnp.arange(momenta, dtype=jnp.int32)
    coord_x = flat_index // (mesh_y * mesh_z)
    coord_y = flat_index // mesh_z % mesh_y
    coord_z = flat_index % mesh_z
    return (coord_x, coord_y, coord_z)


def phase_tables(momenta, mesh_x, mesh_y, mesh_z):
    coord_x, coord_y, coord_z = mesh_coords(momenta, mesh_y, mesh_z)
    phase_index = (
        coord_x[:, None] * coord_x[None, :] * (mesh_y * mesh_z)
        + coord_y[:, None] * coord_y[None, :] * (mesh_x * mesh_z)
        + coord_z[:, None] * coord_z[None, :] * (mesh_x * mesh_y)
    ) % momenta
    angles = phase_index.astype(jnp.float32) * (2.0 * math.pi / momenta)
    cosine = jnp.cos(angles)
    sine_part = jnp.sin(angles)
    forward = jnp.stack([jnp.stack([cosine, sine_part], 1), jnp.stack([-sine_part, cosine], 1)]) * (
        1.0 / momenta
    )
    backward = jnp.stack([jnp.stack([cosine, -sine_part], 1), jnp.stack([sine_part, cosine], 1)])
    return (forward.astype(jnp.bfloat16), backward.astype(jnp.bfloat16))


def pieces_of(values, axis):
    high = lax.reduce_precision(values, 8, 7)
    rest = values - high
    middle = lax.reduce_precision(rest, 8, 7)
    return jnp.concatenate([high, middle, rest - middle], axis=axis).astype(jnp.bfloat16)


def shifted_slots(bond_offsets, sign, sides):
    mesh_x, mesh_y, mesh_z = sides
    coords = mesh_coords(mesh_x * mesh_y * mesh_z, mesh_y, mesh_z)
    slot = 0
    for axis, side in enumerate(sides):
        moved = jnp.mod(coords[axis][None, :] + sign * bond_offsets[:, axis][:, None], side)
        slot = slot * side + moved
    return slot


def shifted_weights(mixing, bond_offsets, column_bonds, row_count, sides):
    count, momenta = mixing.shape
    f32 = jnp.float32
    slots = shifted_slots(bond_offsets, 1, sides)
    source = lax.broadcasted_iota(jnp.int32, (momenta, NB, momenta), 0)
    picks = (source == slots[None]).astype(jnp.bfloat16).reshape(momenta, NB * momenta)
    first = jnp.dot(pieces_of(mixing, 0), picks, preferred_element_type=f32)
    first = first[:count] + first[count : 2 * count] + first[2 * count :]
    first = first.reshape(count * NB, momenta)
    row = lax.broadcasted_iota(jnp.int32, (count * NB, count * LANES), 0)
    lane = lax.broadcasted_iota(jnp.int32, (count * NB, count * LANES), 1)
    spot = lane % LANES
    spread = (row == lane // LANES * NB + spot % NB) & (spot < row_count)
    spread = spread.astype(jnp.bfloat16)
    wide = jnp.dot(pieces_of(first.T, 0), spread, preferred_element_type=f32)
    wide = wide[:momenta] + wide[momenta : 2 * momenta] + wide[2 * momenta :]
    slots = shifted_slots(column_bonds, -1, sides)
    target = lax.broadcasted_iota(jnp.int32, (NB, momenta, momenta), 2)
    picks = (target == slots[:, :, None]).astype(jnp.bfloat16)
    length = NB * row_count
    spans = -(-length // LANES)
    return pl.pallas_call(
        functools.partial(weights_kernel, row_count),
        in_specs=[whole(), whole()],
        out_specs=whole(),
        out_shape=jax.ShapeDtypeStruct((count, momenta, spans * LANES), f32),
        scratch_shapes=[pltpu.VMEM((NB, count, momenta, LANES), f32)],
        compiler_params=pltpu.CompilerParams(vmem_limit_bytes=32 * 1024 * 1024),
    )(picks, pieces_of(wide, 1))


def weights_kernel(row_count, picks_ref, wide_ref, out_ref, tmp_ref):
    count, momenta, _ = out_ref.shape
    width = count * LANES
    spans = out_ref.shape[2] // LANES

    def pick(n, carry):
        both = jnp.dot(picks_ref[n], wide_ref[...], preferred_element_type=jnp.float32)
        both = both[:, :width] + both[:, width : 2 * width] + both[:, 2 * width :]
        for j in range(count):
            tmp_ref[n, j] = both[:, j * LANES : (j + 1) * LANES]
        return carry

    lax.fori_loop(0, NB, pick, 0)
    edge = NB * row_count - (spans - 1) * LANES

    def pack(j, carry):
        for i in range(spans):
            tile = packed(lambda s, _: tmp_ref[s, j], i, NB, row_count)
            if i == spans - 1:
                tile = jnp.where(lane_ids(momenta) < edge, tile, 0.0)
            out_ref[j, :, i * LANES : (i + 1) * LANES] = tile
        return carry

    lax.fori_loop(0, count, pack, 0)


def lane_ids(rows):
    return lax.broadcasted_iota(jnp.int32, (rows, LANES), 1)


def moved(tile, shift):
    shift = shift % LANES
    return pltpu.roll(tile, shift, 1) if shift else tile


def cut(get, start, length, last):
    index, offset = divmod(start, LANES)
    tile = moved(get(index), -offset)
    if offset + length <= LANES or index == last:
        return tile
    rest = moved(get(index + 1), LANES - offset)
    return jnp.where(lane_ids(tile.shape[0]) < LANES - offset, tile, rest)


def packed(get, j, segments, length):
    low, high = j * LANES, (j + 1) * LANES
    out = None
    for s in range(segments):
        for i in range(-(-length // LANES)):
            first = s * length + i * LANES
            stop = s * length + min((i + 1) * LANES, length)
            if stop <= low or first >= high:
                continue
            tile = moved(get(s, i), first - low)
            begin = max(first, low) - low
            out = tile if out is None else jnp.where(lane_ids(tile.shape[0]) < begin, out, tile)
    return out


def spread_kernel(v_hbm, out_hbm, v_ref, tmp_ref, out_ref, in_sems, out_sems):
    channels, mesh_z, row_count, width = v_ref.shape
    groups, tiles, inner, _ = out_ref.shape
    order = width // 2
    narrow = order // groups
    share = groups // PARTS
    arriving = {
        (t, z): pltpu.make_async_copy(v_hbm.at[t, z], v_ref.at[t, z], in_sems.at[t, z])
        for t in range(channels)
        for z in range(mesh_z)
    }
    for copy in arriving.values():
        copy.start()

    for t in range(channels):
        for z in range(mesh_z):
            arriving[t, z].wait()
            block = v_ref[t, z].astype(jnp.float32)
            zeros = jnp.zeros((LANES - row_count, width), jnp.float32)
            turned = jnp.concatenate([block, zeros], axis=0).T
            for p in range(2):
                for n in range(narrow):
                    start = p * order + n * groups
                    tmp_ref[t * narrow + n, pl.ds(2 * z + p, groups, stride=inner), :] = turned[
                        start : start + groups
                    ]

    leaving = []
    for c in range(PARTS):
        part = pl.ds(c * share, share)
        leaving.append(pltpu.make_async_copy(out_ref.at[part], out_hbm.at[part], out_sems.at[c]))
        rows = pl.ds(c * share * inner, share * inner)
        for j in range(tiles):
            tile = packed(lambda s, i: tmp_ref[s, rows], j, channels * narrow, row_count)
            out_ref[part, j] = tile.reshape(share, inner, LANES).astype(jnp.bfloat16)
        leaving[c].start()
    for copy in leaving:
        copy.wait()


def whole():
    return pl.BlockSpec(memory_space=pltpu.VMEM)


def spread_rows(vertex, groups):
    channels, mesh_z, row_count, width = vertex.shape
    narrow = width // 2 // groups
    tiles = -(-channels * narrow * row_count // LANES)
    shape = (groups, tiles, 2 * mesh_z, LANES)
    return pl.pallas_call(
        spread_kernel,
        in_specs=[pl.BlockSpec(memory_space=pltpu.HBM)],
        out_specs=pl.BlockSpec(memory_space=pltpu.HBM),
        out_shape=pltpu.HBM(shape, jnp.bfloat16),
        scratch_shapes=[
            pltpu.VMEM(vertex.shape, jnp.bfloat16),
            pltpu.VMEM((channels * narrow, groups * 2 * mesh_z, LANES), jnp.float32),
            pltpu.VMEM(shape, jnp.bfloat16),
            pltpu.SemaphoreType.DMA((channels, mesh_z)),
            pltpu.SemaphoreType.DMA((PARTS,)),
        ],
        compiler_params=pltpu.CompilerParams(vmem_limit_bytes=32 * 1024 * 1024),
    )(pltpu.with_memory_space_constraint(vertex, pltpu.HBM))


def transform_kernel(
    length, x_ref, forward_ref, backward_ref, w_hbm, out_hbm, lat_ref, mix_ref, out_ref, w_ref, sem, out_sems
):
    f32, bf16 = jnp.float32, jnp.bfloat16
    rows = forward_ref.shape[0]
    tiles = x_ref.shape[1]
    spans = -(-length // LANES)
    copy = pltpu.make_async_copy(w_hbm, w_ref, sem)
    copy.start()

    def x_tile(j):
        return x_ref[:, j].astype(f32).reshape(rows, LANES)

    def by_pairs(step):
        def pair(i, carry):
            step([2 * i, 2 * i + 1])
            return carry

        lax.fori_loop(0, tiles // 2, pair, 0, unroll=True)
        if tiles % 2:
            step([tiles - 1])

    def forward(places):
        x = jnp.concatenate([x_tile(j).astype(bf16) for j in places], axis=1)
        lattice = jnp.dot(forward_ref[...], x, preferred_element_type=f32).astype(bf16)
        for place, j in enumerate(places):
            lat_ref[j] = lattice[:, place * LANES : (place + 1) * LANES]

    by_pairs(forward)
    copy.wait()
    share = rows // PARTS

    def mix(c, carry):
        part = pl.ds(pl.multiple_of(c * share, share), share)
        half = pl.ds(pl.multiple_of(c % (PARTS // 2) * share, share), share)
        mixed = {}
        for i in range(spans):
            lanes = slice(i * LANES, (i + 1) * LANES)
            source = [
                cut(
                    lambda j: lat_ref[j, part].astype(f32),
                    t * length + i * LANES,
                    min(LANES, length - i * LANES),
                    tiles - 1,
                )
                for t in range(3)
            ]
            for t in range(3):
                summed = (
                    w_ref[2 * t, half, lanes] * source[(t + 1) % 3]
                    + w_ref[2 * t + 1, half, lanes] * source[(t + 2) % 3]
                )
                mixed[t, i] = summed.astype(bf16)
        for j in range(tiles):
            tile = packed(lambda t, i: mixed[t, i].astype(f32), j, 3, length)
            mix_ref[j, part] = tile.astype(bf16)
        return carry

    lax.fori_loop(0, PARTS, mix, 0)

    def backward(places):
        mixed = jnp.concatenate([mix_ref[j] for j in places], axis=1)
        projected = jnp.dot(backward_ref[...], mixed, preferred_element_type=f32).astype(bf16)
        for place, j in enumerate(places):
            part = projected[:, place * LANES : (place + 1) * LANES].astype(f32)
            united = (x_tile(j) + part).astype(bf16)
            out_ref[j] = united.reshape(rows // 2, 2, LANES)
            leaving(j).start()

    def leaving(j):
        return pltpu.make_async_copy(out_ref.at[j], out_hbm.at[:, j], out_sems.at[j])

    by_pairs(backward)
    for j in range(tiles):
        leaving(j).wait()


def transform(x, forward, backward, w, length):
    groups, tiles, inner, _ = x.shape
    rows = groups * inner
    return pl.pallas_call(
        functools.partial(transform_kernel, length),
        in_specs=[whole(), whole(), whole(), pl.BlockSpec(memory_space=pl.ANY)],
        out_specs=pl.BlockSpec(memory_space=pltpu.HBM),
        out_shape=pltpu.HBM((rows // 2, tiles, 2, LANES), jnp.bfloat16),
        scratch_shapes=[
            pltpu.VMEM((tiles, rows, LANES), jnp.bfloat16),
            pltpu.VMEM((tiles, rows, LANES), jnp.bfloat16),
            pltpu.VMEM((tiles, rows // 2, 2, LANES), jnp.bfloat16),
            pltpu.VMEM(w.shape, jnp.float32),
            pltpu.SemaphoreType.DMA,
            pltpu.SemaphoreType.DMA((tiles,)),
        ],
        compiler_params=pltpu.CompilerParams(vmem_limit_bytes=28 * 1024 * 1024),
    )(x, forward, backward, pltpu.with_memory_space_constraint(w, pltpu.HBM))


def products_kernel(t, mine_ref, u_ref, loop_hbm, *refs):
    out_refs, (rows_ref, loop_ref, tall_ref, wide_ref, sem) = refs[:-5], refs[-5:]
    f32, bf16 = jnp.float32, jnp.bfloat16
    mine = mine_ref[0]
    tiles = rows_ref.shape[0]
    cols = len(out_refs)
    groups = u_ref.shape[2] // cols
    order = tall_ref.shape[0] // 2
    narrow = order // groups
    depth = cols * LANES
    row_count = out_refs[0].shape[0]
    first = t * narrow * row_count // LANES
    copy = pltpu.make_async_copy(loop_hbm.at[t], loop_ref, sem)
    copy.start()
    rows_ref[...] = u_ref[first : first + tiles].astype(f32)

    def place(k, carry):
        here = pl.ds(pl.multiple_of(k * LANES, LANES), LANES)
        slab = pl.ds(pl.multiple_of((k ^ mine) * LANES, LANES), LANES)
        there = pl.ds(pl.multiple_of(depth + k * LANES, LANES), LANES)
        for n in range(narrow):
            real, imag = [
                cut(
                    lambda j: rows_ref[j, p, pl.ds(k, groups, stride=cols), :],
                    (t * narrow + n) * row_count - first * LANES,
                    row_count,
                    tiles - 1,
                )
                for p in range(2)
            ]
            minus = (-imag).astype(bf16)
            real, imag = real.astype(bf16), imag.astype(bf16)
            upper = slice(n * groups, (n + 1) * groups)
            lower = slice(order + n * groups, order + (n + 1) * groups)
            tall_ref[upper, slab] = real
            tall_ref[lower, slab] = imag
            wide_ref[upper, here] = real
            wide_ref[upper, there] = minus
            wide_ref[lower, here] = imag
            wide_ref[lower, there] = real
        return carry

    lax.fori_loop(0, cols, place, 0)
    copy.wait()
    middle = lax.dot_general(
        tall_ref[...], loop_ref[...], (((0,), (0,)), ((), ())), preferred_element_type=f32
    ).astype(bf16)
    change = lax.dot_general(
        middle, wide_ref[...], (((1,), (1,)), ((), ())), preferred_element_type=f32
    )
    increment = (step_length * change).astype(bf16)
    for k in range(cols):
        out_refs[k][...] = increment[k * LANES : k * LANES + row_count]


def products(t, mine, u, loops, row_count):
    rows, depth = loops.shape[1:]
    cols = depth // 2 // LANES
    length = rows // 2 // (u.shape[2] // cols) * row_count
    tiles = -(-(t + 1) * length // LANES) - t * length // LANES
    return pl.pallas_call(
        functools.partial(products_kernel, t),
        in_specs=[
            pl.BlockSpec(memory_space=pltpu.SMEM),
            whole(),
            pl.BlockSpec(memory_space=pl.ANY),
        ],
        out_specs=[whole()] * cols,
        out_shape=[jax.ShapeDtypeStruct((row_count, rows), jnp.bfloat16)] * cols,
        scratch_shapes=[
            pltpu.VMEM((tiles,) + u.shape[1:], jnp.float32),
            pltpu.VMEM((rows, depth), jnp.bfloat16),
            pltpu.VMEM((rows, depth // 2), jnp.bfloat16),
            pltpu.VMEM((rows, depth), jnp.bfloat16),
            pltpu.SemaphoreType.DMA,
        ],
        compiler_params=pltpu.CompilerParams(vmem_limit_bytes=32 * 1024 * 1024),
    )(mine, u, pltpu.with_memory_space_constraint(loops, pltpu.HBM))


def finish_kernel(t, count, mine_ref, v_ref, *refs):
    piece_refs, out_hbm, (new_ref, sems) = refs[:count], refs[-3], refs[-2:]
    mine = mine_ref[0]
    copies = []
    for k in range(count):
        q = mine ^ k
        total = v_ref[t, q].astype(jnp.float32) + piece_refs[k][...].astype(jnp.float32)
        new_ref[k] = total.astype(jnp.bfloat16)
        copies.append(pltpu.make_async_copy(new_ref.at[k], out_hbm.at[t, q], sems.at[k]))
        copies[k].start()
    for copy in copies:
        copy.wait()


def finish(t, mine, vertex, pieces, out):
    count = len(pieces)
    operands = [mine, vertex, *pieces]
    specs = [
        pl.BlockSpec(memory_space=pltpu.SMEM),
        whole(),
    ] + [whole()] * count
    aliases = {}
    if out is not None:
        aliases = {len(operands): 0}
        operands.append(out)
        specs.append(pl.BlockSpec(memory_space=pltpu.HBM))
    return pl.pallas_call(
        functools.partial(finish_kernel, t, count),
        in_specs=specs,
        out_specs=pl.BlockSpec(memory_space=pltpu.HBM),
        out_shape=jax.ShapeDtypeStruct(vertex.shape, vertex.dtype),
        input_output_aliases=aliases,
        scratch_shapes=[
            pltpu.VMEM((count,) + vertex.shape[2:], vertex.dtype),
            pltpu.SemaphoreType.DMA((count,)),
        ],
        compiler_params=pltpu.CompilerParams(vmem_limit_bytes=16 * 1024 * 1024),
    )(*operands)


def per_device(vertex, loop_blocks, mixing, bond_offsets):
    groups = lax.axis_size("pb")
    cols = lax.axis_size("col")
    mesh_z = vertex.shape[1]
    row_count = vertex.shape[2]
    order = vertex.shape[3] // 2
    narrow = order // groups
    momenta = mesh_z * groups
    mesh_y = groups // MX
    sent = spread_rows(vertex, groups)
    gathered = lax.all_to_all(sent, "pb", split_axis=0, concat_axis=0, tiled=True)

    forward, backward = phase_tables(momenta, MX, mesh_y, mesh_z)
    forward = forward.transpose(2, 3, 1, 0).reshape(2 * momenta, 2 * momenta)
    backward = backward.transpose(3, 2, 0, 1).reshape(2 * momenta, 2 * momenta)
    bond = jnp.arange(NB, dtype=jnp.int32)
    own = (jnp.arange(narrow, dtype=jnp.int32) * groups + lax.axis_index("pb")) % NB
    column_bonds = jnp.sum(
        jnp.where((own[:, None] == bond[None, :])[:, :, None], bond_offsets[None], 0), axis=1
    )
    w = shifted_weights(mixing, bond_offsets, column_bonds, row_count, (MX, mesh_y, mesh_z))
    lane_pad = LANES - row_count
    loops = loop_blocks.reshape(3, order, 2, cols, row_count)
    loops = jnp.pad(loops, [(0, 0)] * 4 + [(0, lane_pad)]).reshape(3, order, 2, cols * LANES)
    loop_re, loop_im = loops[:, :, 0], loops[:, :, 1]
    loops = jnp.concatenate(
        [
            jnp.concatenate([loop_re, loop_im], axis=2),
            jnp.concatenate([-loop_im, loop_re], axis=2),
        ],
        axis=1,
    )

    gathered, loops = lax.optimization_barrier((gathered, loops))
    united = transform(gathered, forward, backward, w, narrow * row_count)
    sent = lax.all_to_all(united, ("pb", "col"), split_axis=0, concat_axis=0, tiled=True)
    u = sent.transpose(1, 2, 0, 3)
    mine = lax.axis_index("col").astype(jnp.int32).reshape(1)
    parts = []
    for t in range(3):
        if t:
            u, parts[0][1] = lax.optimization_barrier((u, parts[0][1]))
        pieces = list(products(t, mine, u, loops, row_count))
        for k in reversed(range(1, cols)):
            pieces[k] = lax.ppermute(pieces[k], "col", [(i, i ^ k) for i in range(cols)])
        parts.append(pieces)
    out = None
    for t in range(3):
        out = finish(t, mine, vertex, parts[t], out)
    return out


def solution(mesh):
    return jax.shard_map(
        per_device,
        mesh=mesh,
        in_specs=(P(None, "pb", "col", None), P(None, ("pb", "col"), None, None), P(), P()),
        out_specs=P(None, "pb", "col", None),
        check_vma=False,
    )
```
